128 devices in a mesh: tile: 8 (over z, core), focus: 16 (over x, y).
Axes of the slice: x: 4, y: 4, z: 4, core: 2. Of those that a mesh axis runs over, the one named last changes fastest.
Arguments:
- mask_tiles: bfloat16 [1024, 512, 512], P(('tile', 'focus')), may hold values from -1 to 1
- class_of_tile: int32 [1024, 1], P(('tile', 'focus')), may hold values from 0 to 15; in each aligned block of 8 rows (0 to 7, 8 to 15, ...) at most 2 rows name the same one
- cell_of_tile: int32 [1024], P(('tile', 'focus')), may hold values from 0 to 1023
- kernels: bfloat16 [16, 24, 4, 4096], P('focus'), may hold values from -0.19921875 to 0.19921875
- class_center: float32 [16], replicated, may hold values from -0.6 to 0.6
Outputs:
- resist_image: bfloat16 [1024, 512, 512], P(('tile', 'focus'))
The draws below stay inside these ranges and needn't reach their ends.
Inputs may be any that keep to these rules, and one draw needn't show every extreme that they name: `class_of_tile`: the 8 tiles of one device hold at most 2 tiles of any one class.
All inputs are finite; a program needn't handle non-finite values.
Results may differ from the reference program's by a relative error of at most 0.009.
Values may be sent and summed in bfloat16 or wider, within the bound.
No kernel may reach another device: no remote copies, remote signals or barrier semaphores. Data moves between devices by JAX's collectives and lax.ppermute only.
A program may use at most 128 MiB of HBM per device.

```python
import math
import jax
import jax.numpy as jnp
import numpy as np
from jax import lax

P_SIZE = 512
NF = 64
KER = 24
BLK_PX = 64
CAP = 2
SC = 32
TILE_DEV = 8
Q = 128
B = 8
SETS = 16
TILES = 1024
NSUP = 1024
REACH = 64


def draw_mask_tiles(key, part):
    scale_key, value_key = jax.random.split(jax.random.fold_in(key, 11))
    levels = jnp.exp(jax.random.uniform(scale_key, (TILES, B, B), jnp.float32, jnp.log(0.1), 0.0))
    levels = jnp.repeat(jnp.repeat(levels, BLK_PX, axis=1), BLK_PX, axis=2)
    values = jax.random.uniform(value_key, (TILES, P_SIZE, P_SIZE), jnp.float32, -1.0, 1.0)
    return (levels * values).astype(jnp.bfloat16)


def set_ends(entries, key, least, largest):
    index_at = [jax.random.randint(jax.random.fold_in(key, axis), (), 0, length) for axis, length in enumerate(entries.shape)]
    main_axis = entries.shape.index(max(entries.shape))
    neighbour = index_at[:main_axis] + [(index_at[main_axis] + 1) % entries.shape[main_axis]] + index_at[main_axis + 1:]
    return entries.at[tuple(index_at)].set(least).at[tuple(neighbour)].set(largest)


def block_levels(rng, dims, cuts, low, high):
    loudness, own = 1.0, jax.random.fold_in(rng, 6)
    for dim, blocks in cuts:
        steps = jnp.exp(jax.random.uniform(jax.random.fold_in(own, dim), (blocks,), jnp.float32, low / len(cuts), high / len(cuts)))
        loudness = loudness * jnp.repeat(steps, dims[dim] // blocks).reshape([-1 if axis == dim else 1 for axis in range(len(dims))])
    return loudness


def shared_out(rng, own, number, rows, number_of, top, bound, lean):
    order = jax.random.permutation(rng, number_of)
    crowded, usual = portions_of(number_of, rows * top, bound, lean, True), portions_of(number_of, rows * top, bound, lean, False)
    places = jnp.arange(number_of)

    def named(tallies, offset_by):
        used = int((tallies > 0).sum())
        fixed = max(1, used // 4)
        moved = fixed + (places - fixed + offset_by * (used - fixed)) % max(1, number_of - fixed)
        return jnp.zeros((number_of,), jnp.int32).at[order[jnp.where(places < fixed, places, moved)]].set(jnp.asarray(tallies, jnp.int32))

    tallies = jnp.where(number % 4 == 0, named(crowded, number // 4), named(usual, number - number // 4 - 1))
    mixed = jax.random.permutation(jax.random.fold_in(own, 3), number_of)
    donor, receiver = mixed[0:number_of // 2 * 2:2], mixed[1:number_of // 2 * 2:2]
    room = jnp.minimum(tallies[donor] - 1, bound - tallies[receiver]) // 2
    room = jnp.where((donor == order[0]) | (receiver == order[0]) | (tallies[receiver] == 0), 0, jnp.maximum(room, 0))
    moved = jax.random.randint(jax.random.fold_in(own, 4), (number_of // 2,), 0, 1 << 20) % (room + 1)
    tallies = tallies.at[donor].add(-moved).at[receiver].add(moved)
    labels = jnp.searchsorted(jnp.cumsum(tallies), jnp.arange(rows * top), side="right").astype(jnp.int32)
    listing = labels.reshape(top, rows).T
    listing = listing[jax.random.permutation(jax.random.fold_in(own, 1), rows)]
    offset_by = jax.random.randint(jax.random.fold_in(own, 2), (rows, 1), 0, top)
    return jnp.take_along_axis(listing, (jnp.arange(top)[None, :] + offset_by) % top, axis=1)


def portions_of(number_of, total, bound, lean, full):
    weights = [(1 << 20) // math.isqrt(grade ** lean) + 1 for grade in range(1, number_of + 1)]
    largest = bound if full else min(bound, max(-(-total // number_of), total * weights[0] // sum(weights)))
    least = 1 if total - largest >= number_of - 1 else 0
    holding, spare = [largest] + [least] * (number_of - 1), total - largest - least * (number_of - 1)
    while spare > 0:
        candidates = [i for i in range(1, number_of) if holding[i] < largest] or [i for i in range(1, number_of) if holding[i] < bound]
        whole, budget = sum([weights[i] for i in candidates]), spare
        for i in candidates:
            addition = min(bound - holding[i], max(1, budget * weights[i] // whole), spare)
            holding[i] = holding[i] + addition
            spare = spare - addition
    return np.array(holding)


def gaussian(rng, shape, scale, limit, pieces=(), held_as=jnp.bfloat16):
    drawn = jax.random.normal(rng, shape, jnp.float32) * scale
    if len(pieces) > 0:
        drawn = block_levels(rng, shape, pieces, -0.22, 0.18) * drawn
    return jnp.clip(drawn, min=-limit, max=limit).astype(held_as)


def setup_inputs(seed: int = 0) -> dict:
    splits = jax.random.split(jax.random.key(seed), 6)
    mask_tiles = draw_mask_tiles(jax.random.fold_in(splits[5], 71), 0)
    class_of_tile_keys = jax.random.split(jax.random.fold_in(splits[1], 1), TILES // TILE_DEV)
    class_of_tile_turns = jax.random.permutation(jax.random.fold_in(splits[1], 3), TILES // TILE_DEV)
    class_of_tile = jax.vmap(lambda own, number: shared_out(jax.random.fold_in(splits[1], 2), own, number, TILE_DEV, SETS, 1, CAP, 2))(class_of_tile_keys, class_of_tile_turns).reshape((TILES, 1))
    cell_of_tile = set_ends(jax.random.randint(splits[2], (TILES,), 0, NSUP), jax.random.fold_in(splits[2], 1), 0, NSUP - 1).astype(jnp.int32)
    kernels = gaussian(splits[3], (SETS, KER, 4, NF * NF), 0.03125, 0.19921875, ((0, 16),))
    class_center = jnp.clip(jax.random.uniform(splits[4], (SETS,), jnp.float32, -0.6, 0.6), -0.6, 0.6)
    return dict(mask_tiles=mask_tiles, class_of_tile=class_of_tile, cell_of_tile=cell_of_tile, kernels=kernels, class_center=class_center)


GAIN_SCALE = 50.0
BEST = lax.Precision.HIGHEST


def spectral_table(freq_count, length):
    frequency = jnp.arange(freq_count, dtype=jnp.int32) - freq_count // 2
    places = jnp.arange(length, dtype=jnp.int32)
    phases = jnp.mod(frequency[:, None] * places[None, :], length).astype(jnp.float32) * (2.0 * jnp.pi / length)
    return jnp.cos(phases), jnp.sin(phases)


def imaging_table(freq_count, samples):
    cosine, sine_part = spectral_table(freq_count, samples)
    upper_rows = jnp.concatenate([cosine, sine_part], axis=1)
    lower_rows = jnp.concatenate([-sine_part, cosine], axis=1)
    return jnp.concatenate([upper_rows, lower_rows], axis=0).astype(jnp.bfloat16)


def resist_table(pixels, samples):
    cos_pix, sin_pix = spectral_table(samples, pixels)
    cos_smp, sin_smp = spectral_table(samples, samples)
    frequency = (jnp.arange(samples, dtype=jnp.int32) - samples // 2).astype(jnp.float32)
    weight = jnp.exp(-0.5 * (frequency * (4.0 / samples)) ** 2)
    combined = jnp.dot((cos_pix * weight[:, None]).T, cos_smp, precision=BEST)
    combined = combined + jnp.dot((sin_pix * weight[:, None]).T, sin_smp, precision=BEST)
    return (combined / samples).astype(jnp.bfloat16)


def spread_table(extent, length):
    places = jnp.arange(extent, dtype=jnp.int32).astype(jnp.float32)
    weight = jnp.exp(-jnp.abs(places[:, None] - places[None, :]) / length)
    return weight / jnp.sum(weight, axis=1, keepdims=True)


def to_map(totals):
    strips = totals.shape[0] // SC
    return totals.reshape(strips, SC, B, B).transpose(0, 2, 1, 3).reshape(strips * B, SC * B)


def cell_means(field_map):
    strips = field_map.shape[0] // B
    return jnp.mean(field_map.reshape(strips, B, SC, B), axis=(1, 3)).reshape(strips * SC)


def split_spectrum(raw_spectrum):
    cos_cos = raw_spectrum[..., :NF, :NF]
    cos_sin = raw_spectrum[..., :NF, NF:]
    sin_cos = raw_spectrum[..., NF:, :NF]
    sin_sin = raw_spectrum[..., NF:, NF:]
    real_part = (cos_cos - sin_sin) / P_SIZE
    imag_part = -(cos_sin + sin_cos) / P_SIZE
    stacked = jnp.stack([real_part, imag_part], axis=-3)
    return stacked.reshape(raw_spectrum.shape[:-2] + (2, NF * NF)).astype(jnp.bfloat16)


def image_one(spectrum, defocus, kernel_set, right_table, left_table):
    spec_parts = spectrum.astype(jnp.float32)
    weights = kernel_set.astype(jnp.float32)
    kern_re = weights[:, 0] + defocus * weights[:, 2]
    kern_im = weights[:, 1] + defocus * weights[:, 3]
    prod_re = kern_re * spec_parts[0] - kern_im * spec_parts[1]
    prod_im = kern_re * spec_parts[1] + kern_im * spec_parts[0]
    stacked = jnp.concatenate([prod_re.reshape(KER, NF, NF), prod_im.reshape(KER, NF, NF)], axis=2)
    stacked = stacked.astype(jnp.bfloat16).reshape(KER * NF, 2 * NF)
    across = jnp.dot(stacked, right_table, preferred_element_type=jnp.float32).astype(jnp.bfloat16)
    across = across.reshape(KER, NF, 2 * Q)
    fields = jnp.einsum("pu,kuv->pkv", left_table[:, :NF], across[:, :, :Q], preferred_element_type=jnp.float32)
    fields = fields + jnp.einsum("pu,kuv->pkv", left_table[:, NF:], across[:, :, Q:], preferred_element_type=jnp.float32)
    return jnp.sum((fields * fields).reshape(2, Q, KER, Q), axis=(0, 2)).reshape(Q * Q) / KER


def reference(mask_tiles, class_of_tile, cell_of_tile, kernels, class_center):
    wave_rows = jnp.concatenate(spectral_table(NF, P_SIZE), axis=0).astype(jnp.bfloat16)
    right_table = imaging_table(NF, Q)
    left_table = right_table.T
    resist_rows = resist_table(P_SIZE, Q)

    def forward_tile(single):
        projected = jnp.dot(single, wave_rows.T, preferred_element_type=jnp.float32).astype(jnp.bfloat16)
        raw_spectrum = jnp.dot(wave_rows, projected, preferred_element_type=jnp.float32)
        squares = single.astype(jnp.float32) ** 2
        density = jnp.sum(squares.reshape(B, BLK_PX, B, BLK_PX), axis=(1, 3)) / (BLK_PX * BLK_PX)
        return split_spectrum(raw_spectrum), density.reshape(B * B)

    spectra, density = lax.map(forward_tile, mask_tiles, batch_size=32)
    totals = jax.ops.segment_sum(density, cell_of_tile, num_segments=NSUP)
    density_map = to_map(totals)
    effective = jnp.dot(spread_table(density_map.shape[0], REACH), density_map, precision=BEST)
    effective = jnp.dot(effective, spread_table(density_map.shape[1], REACH), precision=BEST)
    heights = cell_means(effective)
    classes = class_of_tile[:, 0]
    defocus_all = GAIN_SCALE * (heights[cell_of_tile] - jnp.mean(heights)) - class_center[classes]

    def image_tile(inputs):
        spectrum, defocus, set_id = inputs
        intensity = image_one(spectrum, defocus, kernels[set_id], right_table, left_table)
        intensity = intensity.astype(jnp.bfloat16).reshape(Q, Q)
        half_way = jnp.dot(intensity, resist_rows.T, preferred_element_type=jnp.float32).astype(jnp.bfloat16)
        return jnp.dot(resist_rows, half_way, preferred_element_type=jnp.float32).astype(jnp.bfloat16)

    return lax.map(image_tile, (spectra, defocus_all, classes), batch_size=16)
```

```python
import functools

import jax
import jax.numpy as jnp
import numpy as np
from jax import lax
from jax.experimental import pallas as pl
from jax.experimental.pallas import tpu as pltpu
from jax.sharding import PartitionSpec as P

P_SIZE = 512
NF = 64
KER = 24
BLK_PX = 64
SC = 32
Q = 128
B = 8
REACH = 64
GRID = SC * B
HALF = KER // 2
GROUPS = HALF // 4
TILES = 8
GAIN_SCALE = 50.0
ALL = ("tile", "focus")
BEST = lax.Precision.HIGHEST
F32 = jnp.float32
BF16 = jnp.bfloat16


def spectral_table(freq_count, length):
    frequency = np.arange(freq_count) - freq_count // 2
    phases = np.mod(frequency[:, None] * np.arange(length)[None, :], length) * (2.0 * np.pi / length)
    return np.cos(phases), np.sin(phases)


def wave_table():
    return np.concatenate(spectral_table(NF, P_SIZE), axis=0)


def left_table():
    c, s = spectral_table(NF, Q)
    return np.concatenate(
        [np.concatenate([c.T, -s.T], axis=1), np.concatenate([s.T, c.T], axis=1)], axis=0
    )


def pair_table():
    c, s = spectral_table(NF, Q)
    z = np.zeros((NF, 2 * Q))
    up = np.concatenate([c, s], axis=1)
    down = np.concatenate([-s, c], axis=1)
    return np.block([[up, z], [z, up], [down, z], [z, down]])


def resist_table(pixels, samples):
    cos_pix, sin_pix = spectral_table(samples, pixels)
    cos_smp, sin_smp = spectral_table(samples, samples)
    frequency = np.arange(samples) - samples // 2
    weight = np.exp(-0.5 * (frequency * (4.0 / samples)) ** 2)[:, None]
    return ((cos_pix * weight).T @ cos_smp + (sin_pix * weight).T @ sin_smp) / samples


def spread_table(extent, length):
    places = np.arange(extent)
    weight = np.exp(-np.abs(places[:, None] - places[None, :]) / length)
    return weight / np.sum(weight, axis=1, keepdims=True)


def height_tables():
    spread = spread_table(GRID, REACH)
    rows = spread.reshape(SC, B, SC, B).mean(axis=1)
    cols = spread.reshape(SC, B, SC, B).mean(axis=3)
    row_part = rows.reshape(4, B, SC, B).transpose(2, 3, 1, 0)
    row_part = np.repeat(row_part, SC, axis=3)
    col_part = np.tile(cols, (1, 1, 4))
    return row_part.astype(np.float32), col_part.astype(np.float32)


def as_bf16(table):
    return jnp.asarray(table.astype(np.float32)).astype(BF16)


def analyse_kernel(cell_ref, mask_ref, wave_t_ref, wave_ref, pick_ref, row_ref, col_ref, spec_ref, height_ref):
    t = pl.program_id(0)
    single = mask_ref[0]
    wide = single.astype(F32)
    sums = jnp.sum((wide * wide).reshape(B, BLK_PX, P_SIZE), axis=1)
    density = jnp.dot(sums, pick_ref[...], precision=BEST, preferred_element_type=F32)
    cell = cell_ref[t]
    col = col_ref[cell & (SC - 1)]
    along = jnp.zeros((B, 4 * SC), F32)
    for j in range(B):
        along = along + density[:, j : j + 1] * col[j : j + 1, :]
    row = cell // SC
    part = jnp.zeros((B, 4 * SC), F32)
    for i in range(B):
        part = part + row_ref[row, i] * along[i : i + 1, :]

    @pl.when(t == 0)
    def _():
        height_ref[...] = part

    @pl.when(t > 0)
    def _():
        height_ref[...] += part

    projected = jnp.dot(single, wave_t_ref[...], preferred_element_type=F32).astype(BF16)
    raw = jnp.dot(wave_ref[...], projected, preferred_element_type=F32)
    turned = pltpu.roll(raw, NF, 1)
    scale = 1.0 / P_SIZE
    re = (raw[:NF] - turned[NF:]) * scale
    im = (turned[:NF] + raw[NF:]) * (-scale)
    lower = lax.broadcasted_iota(jnp.int32, (NF, 2 * NF), 1) < NF
    re = jnp.where(lower, re, pltpu.roll(re, NF, 1))
    im = jnp.where(lower, im, pltpu.roll(im, NF, 1))
    spec_ref[0, 0] = re.astype(BF16)
    spec_ref[0, 1] = im.astype(BF16)


def analyse(mask_tiles, cell_of_tile):
    wave = wave_table()
    pick = np.zeros((P_SIZE, 128), np.float32)
    pick[np.arange(P_SIZE), np.arange(P_SIZE) // BLK_PX] = 1.0 / (BLK_PX * BLK_PX)
    row_part, col_part = height_tables()
    fixed = lambda shape: pl.BlockSpec(shape, lambda t: (0,) * len(shape))
    return pl.pallas_call(
        analyse_kernel,
        grid=(TILES,),
        in_specs=[
            pl.BlockSpec(memory_space=pltpu.SMEM),
            pl.BlockSpec((1, P_SIZE, P_SIZE), lambda t: (t, 0, 0)),
            fixed((P_SIZE, 2 * NF)),
            fixed((2 * NF, P_SIZE)),
            fixed((P_SIZE, 128)),
            fixed((SC, B, B, 4 * SC)),
            fixed((SC, B, 4 * SC)),
        ],
        out_specs=[
            pl.BlockSpec((1, 2, NF, 2 * NF), lambda t: (t, 0, 0, 0)),
            fixed((B, 4 * SC)),
        ],
        out_shape=[
            jax.ShapeDtypeStruct((TILES, 2, NF, 2 * NF), BF16),
            jax.ShapeDtypeStruct((B, 4 * SC), F32),
        ],
        cost_estimate=pl.CostEstimate(flops=3 * 10**9, bytes_accessed=6 * 10**6, transcendentals=0),
    )(
        cell_of_tile,
        mask_tiles,
        as_bf16(wave.T),
        as_bf16(wave),
        jnp.asarray(pick),
        jnp.asarray(row_part),
        jnp.asarray(col_part),
    )


def image_kernel(
    place_ref, class_ref, cell_ref, centre_ref, height_ref, spec_ref, left_ref, pair_ref,
    own_ref, before_ref, after_ref, far_a_ref, far_b_ref, out_ref, held, sems,
):
    t = pl.program_id(0)
    slot = t & 1

    def fetch(tile, into):
        set_id = class_ref[tile]
        first = (place_ref[0] - (set_id // place_ref[2])) & 3
        second = (place_ref[1] - (set_id // place_ref[3])) & 3

        def from_ref(ref, index):
            pltpu.make_async_copy(ref.at[index], held.at[into], sems.at[into]).start()

        @pl.when(second == 0)
        def _():
            from_ref(own_ref, first)

        @pl.when(second == 1)
        def _():
            from_ref(before_ref, first)

        @pl.when(second == 3)
        def _():
            from_ref(after_ref, first)

        @pl.when((second == 2) & (first < 2))
        def _():
            from_ref(far_a_ref, first & 1)

        @pl.when((second == 2) & (first >= 2))
        def _():
            from_ref(far_b_ref, first & 1)

    @pl.when(t == 0)
    def _():
        fetch(0, 0)

    @pl.when(t + 1 < TILES)
    def _():
        fetch(t + 1, 1 - slot)

    cell = cell_ref[t]
    row = cell // SC
    heights = height_ref[...]
    here = (lax.broadcasted_iota(jnp.int32, heights.shape, 0) == (row & 7)) & (
        lax.broadcasted_iota(jnp.int32, heights.shape, 1) == (row // 8) * SC + (cell & (SC - 1))
    )
    shift = jnp.sum(jnp.where(here, heights, 0.0) - heights * (1.0 / (SC * SC)), keepdims=True)
    shift = GAIN_SCALE * shift - centre_ref[class_ref[t]]

    re_part = spec_ref[0, 0].astype(F32)
    im_part = spec_ref[0, 1].astype(F32)
    re_part = jnp.concatenate([re_part, re_part], axis=1)
    im_part = jnp.concatenate([im_part, im_part], axis=1)
    pltpu.make_async_copy(own_ref.at[0], held.at[slot], sems.at[slot]).wait()
    total = jnp.zeros((Q, Q), F32)
    for g in range(GROUPS):
        kern_re = held[slot, g, 0].astype(F32) + shift * held[slot, g, 2].astype(F32)
        kern_im = held[slot, g, 1].astype(F32) + shift * held[slot, g, 3].astype(F32)
        prod_re = kern_re * re_part - kern_im * im_part
        prod_im = kern_re * im_part + kern_im * re_part
        filtered = jnp.concatenate([prod_re.astype(BF16), prod_im.astype(BF16)], axis=0)
        along = jnp.dot(left_ref[...], filtered, preferred_element_type=F32).astype(BF16)
        for pair in range(2):
            lanes = slice(2 * NF * pair, 2 * NF * (pair + 1))
            both = jnp.concatenate([along[:Q, lanes], along[Q:, lanes]], axis=1)
            fields = jnp.dot(both, pair_ref[...], preferred_element_type=F32)
            for part in range(4):
                block = fields[:, part * Q : (part + 1) * Q]
                total = total + block * block
    out_ref[0] = total.astype(out_ref.dtype)


def image(place, classes, cells, centre, heights, spectra, pieces, dtype):
    smem = pl.BlockSpec(memory_space=pltpu.SMEM)
    anywhere = pl.BlockSpec(memory_space=pl.ANY)
    fixed = lambda shape: pl.BlockSpec(shape, lambda t: (0,) * len(shape))
    return pl.pallas_call(
        image_kernel,
        grid=(TILES,),
        in_specs=[
            smem, smem, smem, smem,
            fixed((B, 4 * SC)),
            pl.BlockSpec((1, 2, NF, 2 * NF), lambda t: (t, 0, 0, 0)),
            fixed((2 * Q, 2 * NF)),
            fixed((4 * NF, 4 * Q)),
            anywhere, anywhere, anywhere, anywhere, anywhere,
        ],
        out_specs=pl.BlockSpec((1, Q, Q), lambda t: (t, 0, 0)),
        out_shape=jax.ShapeDtypeStruct((TILES, Q, Q), dtype),
        scratch_shapes=[
            pltpu.VMEM((2, GROUPS, 4, NF, 4 * NF), BF16),
            pltpu.SemaphoreType.DMA((2,)),
        ],
        cost_estimate=pl.CostEstimate(flops=4 * 10**9, bytes_accessed=5 * 10**6, transcendentals=0),
    )(place, classes, cells, centre, heights, spectra, as_bf16(left_table()), as_bf16(pair_table()), *pieces)


def resist_kernel(own_ref, other_ref, resist_ref, resist_t_ref, out_ref):
    intensity = (own_ref[0] + other_ref[0].astype(F32)) * (1.0 / KER)
    half_way = jnp.dot(intensity.astype(BF16), resist_t_ref[...], preferred_element_type=F32)
    out_ref[0] = jnp.dot(
        resist_ref[...], half_way.astype(BF16), preferred_element_type=F32
    ).astype(BF16)


def resist(own, other):
    table = resist_table(P_SIZE, Q)
    fixed = lambda shape: pl.BlockSpec(shape, lambda t: (0,) * len(shape))
    return pl.pallas_call(
        resist_kernel,
        grid=(TILES,),
        in_specs=[
            pl.BlockSpec((1, Q, Q), lambda t: (t, 0, 0)),
            pl.BlockSpec((1, Q, Q), lambda t: (t, 0, 0)),
            fixed((P_SIZE, Q)),
            fixed((Q, P_SIZE)),
        ],
        out_specs=pl.BlockSpec((1, P_SIZE, P_SIZE), lambda t: (t, 0, 0)),
        out_shape=jax.ShapeDtypeStruct((TILES, P_SIZE, P_SIZE), BF16),
        cost_estimate=pl.CostEstimate(flops=10**9, bytes_accessed=5 * 10**6, transcendentals=0),
    )(own, other, as_bf16(table), as_bf16(table.T))


PLACES = [(z, core, x, y) for z in range(4) for core in range(2) for x in range(4) for y in range(4)]


def place_of(z, core, x, y):
    return ((z * 2 + core) * 4 + x % 4) * 4 + y % 4


def ring(phase, step):
    pairs = []
    for z, core, x, y in PLACES:
        along_y = (core + phase) % 2 == 0
        to = (z, core, x, y + step) if along_y else (z, core, x + step, y)
        pairs.append((place_of(z, core, x, y), place_of(*to)))
    return pairs


def partner(x):
    return lax.ppermute(x, "tile", [(t, t ^ 1) for t in range(8)])


def gather_kernels(mine):
    send = lambda value, phase, step: lax.ppermute(value, ALL, ring(phase, step))
    before = send(mine, 0, 1)
    after = send(mine, 0, -1)
    far_a = send(before[:, :2], 0, 1)
    far_b = send(after[:, 2:], 0, -1)
    line = jnp.stack([mine, before, jnp.concatenate([far_a, far_b], axis=1), after])
    before = send(line, 1, 1)
    after = send(line, 1, -1)
    far_a = send(before[:2], 1, 1)
    far_b = send(after[2:], 1, -1)
    return line, before, after, far_a, far_b


def summed(x, axis):
    size = lax.axis_size(axis)
    copies = jnp.broadcast_to(x[None], (size, *x.shape))
    return jnp.sum(lax.all_to_all(copies, axis, 0, 0, tiled=True), axis=0)


def per_device(mask_tiles, class_of_tile, cell_of_tile, kernels, class_center):
    core = lax.axis_index("tile") % 2
    focus = lax.axis_index("focus")
    x, y = focus // 4, focus % 4
    mine = lax.dynamic_slice_in_dim(kernels[0], core * HALF, HALF, 0)
    mine = mine.reshape(GROUPS, 4, 4, NF, NF).transpose(0, 2, 3, 1, 4).reshape(GROUPS, 4, NF, 4 * NF)
    pieces = gather_kernels(mine)
    place = jnp.stack(
        [
            jnp.where(core == 0, y, x),
            jnp.where(core == 0, x, y),
            jnp.where(core == 0, 1, 4),
            jnp.where(core == 0, 4, 1),
        ]
    ).astype(jnp.int32)

    classes = class_of_tile[:, 0]
    labels = jnp.concatenate([classes, cell_of_tile])
    other_labels = partner(labels)
    spectra, heights = analyse(mask_tiles, cell_of_tile)
    other_spectra = partner(spectra)
    heights = summed(summed(heights, "tile"), "focus")

    part = image(
        place, other_labels[:TILES], other_labels[TILES:], class_center, heights, other_spectra, pieces, BF16
    )
    received = partner(part)
    own = image(place, classes, cell_of_tile, class_center, heights, spectra, pieces, F32)
    return resist(own, received)


def solution(mesh):
    placed = (
        P(("tile", "focus"), None, None),
        P(("tile", "focus"), None),
        P(("tile", "focus")),
        P("focus", None, None, None),
        P(),
    )
    return jax.shard_map(
        per_device,
        mesh=mesh,
        in_specs=placed,
        out_specs=P(("tile", "focus"), None, None),
        check_vma=False,
    )
```

```python
import functools

import jax
import jax.numpy as jnp
import numpy as np
from jax import lax
from jax.experimental import pallas as pl
from jax.experimental.pallas import tpu as pltpu
from jax.sharding import PartitionSpec as P

P_SIZE = 512
NF = 64
KER = 24
BLK_PX = 64
SC = 32
Q = 128
B = 8
REACH = 64
GRID = SC * B
HALF = KER // 2
GROUPS = HALF // 4
TILES = 8
GAIN_SCALE = 50.0
ALL = ("tile", "focus")
BEST = lax.Precision.HIGHEST
F32 = jnp.float32
BF16 = jnp.bfloat16


def spectral_table(freq_count, length):
    frequency = np.arange(freq_count) - freq_count // 2
    phases = np.mod(frequency[:, None] * np.arange(length)[None, :], length) * (2.0 * np.pi / length)
    return np.cos(phases), np.sin(phases)


def wave_table():
    return np.concatenate(spectral_table(NF, P_SIZE), axis=0)


def left_table():
    c, s = spectral_table(NF, Q)
    return np.concatenate(
        [np.concatenate([c.T, -s.T], axis=1), np.concatenate([s.T, c.T], axis=1)], axis=0
    )


def pair_table():
    c, s = spectral_table(NF, Q)
    z = np.zeros((NF, 2 * Q))
    up = np.concatenate([c, s], axis=1)
    down = np.concatenate([-s, c], axis=1)
    return np.block([[up, z], [z, up], [down, z], [z, down]])


def resist_table(pixels, samples):
    cos_pix, sin_pix = spectral_table(samples, pixels)
    cos_smp, sin_smp = spectral_table(samples, samples)
    frequency = np.arange(samples) - samples // 2
    weight = np.exp(-0.5 * (frequency * (4.0 / samples)) ** 2)[:, None]
    return ((cos_pix * weight).T @ cos_smp + (sin_pix * weight).T @ sin_smp) / samples


def spread_table(extent, length):
    places = np.arange(extent)
    weight = np.exp(-np.abs(places[:, None] - places[None, :]) / length)
    return weight / np.sum(weight, axis=1, keepdims=True)


def height_tables():
    spread = spread_table(GRID, REACH)
    rows = spread.reshape(SC, B, SC, B).mean(axis=1)
    cols = spread.reshape(SC, B, SC, B).mean(axis=3)
    row_part = rows.reshape(4, B, SC, B).transpose(2, 3, 1, 0)
    row_part = np.repeat(row_part, SC, axis=3)
    col_part = np.tile(cols, (1, 1, 4))
    return row_part.astype(np.float32), col_part.astype(np.float32)


def as_bf16(table):
    return jnp.asarray(table.astype(np.float32)).astype(BF16)


def fixed(*shape):
    return pl.BlockSpec(shape, lambda *_: (0,) * len(shape))


def tiles(count, *shape):
    return pl.BlockSpec((count, *shape), lambda t: (t,) + (0,) * len(shape))


SMEM = pl.BlockSpec(memory_space=pltpu.SMEM)
VMEM = pl.BlockSpec(memory_space=pltpu.VMEM)
ANY = pl.BlockSpec(memory_space=pl.ANY)


def density_kernel(count, cell_ref, mask_ref, pick_ref, row_ref, col_ref, height_ref):
    step = pl.program_id(0)
    part = jnp.zeros((B, 4 * SC), F32)
    for t in range(count):
        wide = mask_ref[t].astype(F32)
        sums = jnp.sum((wide * wide).reshape(B, BLK_PX, P_SIZE), axis=1)
        density = jnp.dot(sums, pick_ref[...], precision=BEST, preferred_element_type=F32)
        cell = cell_ref[step * count + t]
        col = col_ref[cell & (SC - 1)]
        along = jnp.zeros((B, 4 * SC), F32)
        for j in range(B):
            along = along + density[:, j : j + 1] * col[j : j + 1, :]
        row = cell // SC
        for i in range(B):
            part = part + row_ref[row, i] * along[i : i + 1, :]

    @pl.when(step == 0)
    def _():
        height_ref[...] = part

    @pl.when(step > 0)
    def _():
        height_ref[...] += part


def density_heights(mask_tiles, cell_of_tile, count=2):
    pick = np.zeros((P_SIZE, 128), np.float32)
    pick[np.arange(P_SIZE), np.arange(P_SIZE) // BLK_PX] = 1.0 / (BLK_PX * BLK_PX)
    row_part, col_part = height_tables()
    return pl.pallas_call(
        functools.partial(density_kernel, count),
        grid=(TILES // count,),
        in_specs=[
            SMEM,
            tiles(count, P_SIZE, P_SIZE),
            fixed(P_SIZE, 128),
            fixed(SC, B, B, 4 * SC),
            fixed(SC, B, 4 * SC),
        ],
        out_specs=fixed(B, 4 * SC),
        out_shape=jax.ShapeDtypeStruct((B, 4 * SC), F32),
        name="density",
        cost_estimate=pl.CostEstimate(flops=10**7, bytes_accessed=6 * 10**6, transcendentals=0),
    )(cell_of_tile, mask_tiles, jnp.asarray(pick), jnp.asarray(row_part), jnp.asarray(col_part))


def spectra_kernel(count, mask_ref, wave_t_ref, wave_ref, spec_ref):
    lower = lax.broadcasted_iota(jnp.int32, (NF, 2 * NF), 1) < NF
    scale = 1.0 / P_SIZE
    for t in range(count):
        projected = jnp.dot(mask_ref[t], wave_t_ref[...], preferred_element_type=F32).astype(BF16)
        raw = jnp.dot(wave_ref[...], projected, preferred_element_type=F32)
        turned = pltpu.roll(raw, NF, 1)
        re = (raw[:NF] - turned[NF:]) * scale
        im = (turned[:NF] + raw[NF:]) * (-scale)
        spec_ref[t, 0] = jnp.where(lower, re, pltpu.roll(re, NF, 1)).astype(BF16)
        spec_ref[t, 1] = jnp.where(lower, im, pltpu.roll(im, NF, 1)).astype(BF16)


def form_spectra(mask_tiles, count=2):
    wave = wave_table()
    return pl.pallas_call(
        functools.partial(spectra_kernel, count),
        grid=(TILES // count,),
        in_specs=[tiles(count, P_SIZE, P_SIZE), fixed(P_SIZE, 2 * NF), fixed(2 * NF, P_SIZE)],
        out_specs=tiles(count, 2, NF, 2 * NF),
        out_shape=jax.ShapeDtypeStruct((TILES, 2, NF, 2 * NF), BF16),
        name="spectra",
        cost_estimate=pl.CostEstimate(flops=10**9, bytes_accessed=5 * 10**6, transcendentals=0),
    )(mask_tiles, as_bf16(wave.T), as_bf16(wave))


def image_kernel(
    groups, started, place_ref, class_ref, cell_ref, centre_ref, height_ref, spec_ref, left_ref, pair_ref, *rest
):
    pieces, rest = rest[:5], rest[5:]
    begun_ref = rest[0] if started else None
    out_ref, held, sems = rest[-3:]

    def fetch(tile, into):
        set_id = class_ref[tile]
        first = (place_ref[0] - (set_id // place_ref[2])) & 3
        second = (place_ref[1] - (set_id // place_ref[3])) & 3
        far = (second == 2) & (first < 2)
        cases = (
            (second == 0, first),
            (second == 1, first),
            (second == 3, first),
            (far, first & 1),
            ((second == 2) & (first >= 2), first & 1),
        )
        for ref, (chosen, index) in zip(pieces, cases):

            @pl.when(chosen)
            def _():
                pltpu.make_async_copy(ref.at[index], held.at[into], sems.at[into]).start()

    fetch(0, 0)
    heights = height_ref[...]
    mean = jnp.sum(heights, keepdims=True) * (1.0 / (SC * SC))

    def one_tile(t, carry):
        slot = t & 1

        @pl.when(t + 1 < TILES)
        def _():
            fetch(t + 1, 1 - slot)

        cell = cell_ref[t]
        row = cell // SC
        here = (lax.broadcasted_iota(jnp.int32, heights.shape, 0) == (row & 7)) & (
            lax.broadcasted_iota(jnp.int32, heights.shape, 1) == (row // 8) * SC + (cell & (SC - 1))
        )
        shift = jnp.sum(jnp.where(here, heights, 0.0), keepdims=True) - mean
        shift = GAIN_SCALE * shift - centre_ref[class_ref[t]]
        re_part = spec_ref[t, 0].astype(F32)
        im_part = spec_ref[t, 1].astype(F32)
        re_part = jnp.concatenate([re_part, re_part], axis=1)
        im_part = jnp.concatenate([im_part, im_part], axis=1)
        pltpu.make_async_copy(pieces[0].at[0], held.at[slot], sems.at[slot]).wait()
        filtered = []
        for g in range(groups):
            kern_re = held[slot, g, 0].astype(F32) + shift * held[slot, g, 2].astype(F32)
            kern_im = held[slot, g, 1].astype(F32) + shift * held[slot, g, 3].astype(F32)
            prod_re = kern_re * re_part - kern_im * im_part
            prod_im = kern_re * im_part + kern_im * re_part
            filtered.append(jnp.concatenate([prod_re.astype(BF16), prod_im.astype(BF16)], axis=0))
        along = jnp.dot(
            left_ref[...], jnp.concatenate(filtered, axis=1), preferred_element_type=F32
        ).astype(BF16)
        both = [
            jnp.concatenate([along[:Q, at : at + 2 * NF], along[Q:, at : at + 2 * NF]], axis=1)
            for at in range(0, groups * 4 * NF, 2 * NF)
        ]
        fields = jnp.dot(jnp.concatenate(both, axis=0), pair_ref[...], preferred_element_type=F32)
        total = begun_ref[t] if started else jnp.zeros((Q, Q), F32)
        for part in range(4):
            for at in range(0, groups * 2 * Q, Q):
                block = fields[at : at + Q, part * Q : (part + 1) * Q]
                total = total + block * block
        out_ref[t] = total.astype(out_ref.dtype)
        return carry

    lax.fori_loop(0, TILES, one_tile, 0)


def image(place, classes, cells, centre, heights, spectra, pieces, begun, dtype):
    groups = pieces[0].shape[1]
    started = begun is not None
    return pl.pallas_call(
        functools.partial(image_kernel, groups, started),
        in_specs=[SMEM] * 4 + [VMEM] * 4 + [ANY] * 5 + [VMEM] * started,
        out_specs=VMEM,
        out_shape=jax.ShapeDtypeStruct((TILES, Q, Q), dtype),
        scratch_shapes=[
            pltpu.VMEM((2, groups, 4, NF, 4 * NF), BF16),
            pltpu.SemaphoreType.DMA((2,)),
        ],
        name="image",
        cost_estimate=pl.CostEstimate(
            flops=groups * 10**9, bytes_accessed=(groups + 1) * 10**6, transcendentals=0
        ),
    )(
        place, classes, cells, centre, heights, spectra, as_bf16(left_table()), as_bf16(pair_table()),
        *pieces, *([begun] if started else [])
    )


def resist_kernel(count, own_ref, other_ref, resist_ref, resist_t_ref, out_ref):
    intensity = (own_ref[...] + other_ref[...].astype(F32)) * (1.0 / KER)
    intensity = intensity.astype(BF16).reshape(count * Q, Q)
    half_way = jnp.dot(intensity, resist_t_ref[...], preferred_element_type=F32).astype(BF16)
    for t in range(count):
        out_ref[t] = jnp.dot(
            resist_ref[...], half_way[t * Q : (t + 1) * Q], preferred_element_type=F32
        ).astype(BF16)


def resist(own, other, count=4):
    table = resist_table(P_SIZE, Q)
    return pl.pallas_call(
        functools.partial(resist_kernel, count),
        grid=(TILES // count,),
        in_specs=[tiles(count, Q, Q), tiles(count, Q, Q), fixed(P_SIZE, Q), fixed(Q, P_SIZE)],
        out_specs=tiles(count, P_SIZE, P_SIZE),
        out_shape=jax.ShapeDtypeStruct((TILES, P_SIZE, P_SIZE), BF16),
        name="resist",
        cost_estimate=pl.CostEstimate(flops=10**9, bytes_accessed=5 * 10**6, transcendentals=0),
    )(own, other, as_bf16(table), as_bf16(table.T))


PLACES = [(z, core, x, y) for z in range(4) for core in range(2) for x in range(4) for y in range(4)]
CHUNKS = ((0, 2), (2, 3))


def place_of(z, core, x, y):
    return ((z * 2 + core) * 4 + x % 4) * 4 + y % 4


def ring(phase, step):
    pairs = []
    for z, core, x, y in PLACES:
        along_y = (core + phase) % 2 == 0
        to = (z, core, x, y + step) if along_y else (z, core, x + step, y)
        pairs.append((place_of(z, core, x, y), place_of(*to)))
    return pairs


def send(value, phase, step):
    return lax.ppermute(value, ALL, ring(phase, step))


def after_all(value, *others):
    return lax.optimization_barrier((value, *others))[0]


def partner(x):
    return lax.ppermute(x, "tile", [(t, t ^ 1) for t in range(8)])


def summed(x, axis):
    size = lax.axis_size(axis)
    copies = jnp.broadcast_to(x[None], (size, *x.shape))
    return jnp.sum(lax.all_to_all(copies, axis, 0, 0, tiled=True), axis=0)


def per_device(mask_tiles, class_of_tile, cell_of_tile, kernels, class_center):
    core = lax.axis_index("tile") % 2
    focus = lax.axis_index("focus")
    x, y = focus // 4, focus % 4
    place = jnp.stack(
        [
            jnp.where(core == 0, y, x),
            jnp.where(core == 0, x, y),
            jnp.where(core == 0, 1, 4),
            jnp.where(core == 0, 4, 1),
        ]
    ).astype(jnp.int32)
    classes = class_of_tile[:, 0]
    other_labels = partner(jnp.concatenate([classes, cell_of_tile]))

    mine = lax.dynamic_slice_in_dim(kernels[0], core * HALF, HALF, 0)
    mine = mine.reshape(GROUPS, 4, 4, NF, NF).transpose(0, 2, 3, 1, 4).reshape(GROUPS, 4, NF, 4 * NF)
    before = send(mine, 0, 1)
    after = send(mine, 0, -1)
    heights = density_heights(mask_tiles, cell_of_tile)
    far_a = send(after_all(before[:, :2], heights), 0, 1)
    far_b = send(after_all(after[:, 2:], heights), 0, -1)
    lines = [
        jnp.stack(
            [
                mine[lo:hi],
                before[lo:hi],
                jnp.concatenate([far_a[lo:hi], far_b[lo:hi]], axis=1),
                after[lo:hi],
            ]
        )
        for lo, hi in CHUNKS
    ]
    heights = summed(heights, "tile")
    spectra = form_spectra(mask_tiles)
    other_spectra = partner(spectra)
    nears = [(send(line, 1, 1), send(line, 1, -1)) for line in lines]
    heights = summed(heights, "focus")
    pieces = []
    for line, (before, after) in zip(lines, nears):
        far_a = send(after_all(before[:2], heights), 1, 1)
        far_b = send(after_all(after[2:], heights), 1, -1)
        pieces.append((line, before, after, far_a, far_b))

    own, other = None, None
    for at, chunk in enumerate(pieces):
        last = at + 1 == len(pieces)
        pair_spectra = other_spectra if own is None else after_all(other_spectra, own)
        other = image(
            place, other_labels[:TILES], other_labels[TILES:], class_center, heights, pair_spectra,
            chunk, other, BF16 if last else F32,
        )
        if last:
            other = partner(other)
        own = image(place, classes, cell_of_tile, class_center, heights, spectra, chunk, own, F32)
    return resist(own, other)


def solution(mesh):
    placed = (
        P(("tile", "focus"), None, None),
        P(("tile", "focus"), None),
        P(("tile", "focus")),
        P("focus", None, None, None),
        P(),
    )
    return jax.shard_map(
        per_device,
        mesh=mesh,
        in_specs=placed,
        out_specs=P(("tile", "focus"), None, None),
        check_vma=False,
    )
```

```python
import functools

import jax
import jax.numpy as jnp
import numpy as np
from jax import lax
from jax.experimental import pallas as pl
from jax.experimental.pallas import tpu as pltpu
from jax.sharding import PartitionSpec as P


P_SIZE = 512
NF = 64
KER = 24
BLK_PX = 64
SC = 32
Q = 128
B = 8
REACH = 64
GRID = SC * B
HALF = KER // 2
GROUPS = HALF // 4
TILES = 8
GAIN_SCALE = 50.0
ALL = ("tile", "focus")
BEST = lax.Precision.HIGHEST
F32 = jnp.float32
BF16 = jnp.bfloat16


def spectral_table(freq_count, length):
    frequency = np.arange(freq_count) - freq_count // 2
    phases = np.mod(frequency[:, None] * np.arange(length)[None, :], length) * (2.0 * np.pi / length)
    return np.cos(phases), np.sin(phases)


def wave_table():
    return np.concatenate(spectral_table(NF, P_SIZE), axis=0)


def left_table():
    c, s = spectral_table(NF, Q)
    return np.concatenate(
        [np.concatenate([c.T, -s.T], axis=1), np.concatenate([s.T, c.T], axis=1)], axis=0
    )


def pair_table():
    c, s = spectral_table(NF, Q)
    z = np.zeros((NF, 2 * Q))
    up = np.concatenate([c, s], axis=1)
    down = np.concatenate([-s, c], axis=1)
    return np.block([[up, z], [z, up], [down, z], [z, down]])


def resist_table(pixels, samples):
    cos_pix, sin_pix = spectral_table(samples, pixels)
    cos_smp, sin_smp = spectral_table(samples, samples)
    frequency = np.arange(samples) - samples // 2
    weight = np.exp(-0.5 * (frequency * (4.0 / samples)) ** 2)[:, None]
    return ((cos_pix * weight).T @ cos_smp + (sin_pix * weight).T @ sin_smp) / samples


def spread_table(extent, length):
    places = np.arange(extent)
    weight = np.exp(-np.abs(places[:, None] - places[None, :]) / length)
    return weight / np.sum(weight, axis=1, keepdims=True)


def height_tables():
    spread = spread_table(GRID, REACH)
    rows = spread.reshape(SC, B, SC, B).mean(axis=1)
    cols = spread.reshape(SC, B, SC, B).mean(axis=3)
    row_part = np.tile(rows.transpose(1, 2, 0), (1, 1, 4))
    col_part = np.tile(cols, (1, 1, 4)) / (BLK_PX * BLK_PX)
    return row_part.astype(np.float32), col_part.astype(np.float32)


def as_bf16(table):
    return jnp.asarray(table.astype(np.float32)).astype(BF16)


def fixed(*shape):
    return pl.BlockSpec(shape, lambda *_: (0,) * len(shape))


def tiles(count, *shape):
    return pl.BlockSpec((count, *shape), lambda t: (t,) + (0,) * len(shape))


SMEM = pl.BlockSpec(memory_space=pltpu.SMEM)
VMEM = pl.BlockSpec(memory_space=pltpu.VMEM)
ANY = pl.BlockSpec(memory_space=pl.ANY)


def analyse_kernel(cell_ref, mask_hbm, wave_t_ref, wave_ref, row_ref, col_ref, spec_ref, height_ref, mask, rows, along, sems):
    def copy(t):
        return pltpu.make_async_copy(mask_hbm.at[t], mask.at[t], sems.at[t])

    for t in range(TILES):
        copy(t).start()
    lower = lax.broadcasted_iota(jnp.int32, (NF, 2 * NF), 1) < NF
    left = lax.broadcasted_iota(jnp.int32, (B, 2 * BLK_PX), 1) < BLK_PX
    scale = 1.0 / P_SIZE

    def some_tiles(trip, carry):
        batch = [trip * 2, trip * 2 + 1]
        for t in batch:
            copy(t).wait()
        for t in batch:
            cell = cell_ref[t]
            at = pl.ds(pl.multiple_of(t * B, B), B)
            col = col_ref[cell & (SC - 1)]
            wide = mask[t].astype(F32)
            sums = jnp.sum((wide * wide).reshape(B, BLK_PX, P_SIZE), axis=1)
            spread = jnp.zeros((B, 4 * SC), F32)
            for pair in range(B // 2):
                two = sums[:, pair * 2 * BLK_PX : (pair + 1) * 2 * BLK_PX]
                first = jnp.sum(jnp.where(left, two, 0.0), axis=1, keepdims=True)
                second = jnp.sum(jnp.where(left, 0.0, two), axis=1, keepdims=True)
                spread = spread + first * col[2 * pair : 2 * pair + 1] + second * col[2 * pair + 1 : 2 * pair + 2]
            along[at, :] = spread
            rows[at, :] = row_ref[cell // SC]
        for t in batch:
            projected = jnp.dot(mask[t], wave_t_ref[...], preferred_element_type=F32).astype(BF16)
            raw = jnp.dot(wave_ref[...], projected, preferred_element_type=F32)
            turned = pltpu.roll(raw, NF, 1)
            re = (raw[:NF] - turned[NF:]) * scale
            im = (turned[:NF] + raw[NF:]) * (-scale)
            spec_ref[t, 0] = jnp.where(lower, re, pltpu.roll(re, NF, 1)).astype(BF16)
            spec_ref[t, 1] = jnp.where(lower, im, pltpu.roll(im, NF, 1)).astype(BF16)
        return carry

    lax.fori_loop(0, TILES // 2, some_tiles, 0)
    whole = lax.dot_general(
        rows[...], along[...], (((0,), (0,)), ((), ())), precision=BEST, preferred_element_type=F32
    )
    quarter = lax.broadcasted_iota(jnp.int32, (B, 4 * SC), 1) // SC
    part = jnp.zeros((B, 4 * SC), F32)
    for q in range(4):
        part = jnp.where(quarter == q, whole[q * B : (q + 1) * B], part)
    height_ref[...] = part


def analyse(mask_tiles, cell_of_tile):
    wave = wave_table()
    row_part, col_part = height_tables()
    return pl.pallas_call(
        analyse_kernel,
        in_specs=[SMEM, ANY] + [VMEM] * 4,
        out_specs=[VMEM, VMEM],
        out_shape=[
            jax.ShapeDtypeStruct((TILES, 2, NF, 2 * NF), BF16),
            jax.ShapeDtypeStruct((B, 4 * SC), F32),
        ],
        scratch_shapes=[
            pltpu.VMEM((TILES, P_SIZE, P_SIZE), BF16),
            pltpu.VMEM((TILES * B, 4 * SC), F32),
            pltpu.VMEM((TILES * B, 4 * SC), F32),
            pltpu.SemaphoreType.DMA((TILES,)),
        ],
        name="analyse",
        cost_estimate=pl.CostEstimate(flops=10**9, bytes_accessed=6 * 10**6, transcendentals=0),
    )(cell_of_tile, mask_tiles, as_bf16(wave.T), as_bf16(wave), jnp.asarray(row_part), jnp.asarray(col_part))


def image_kernel(
    place_ref, class_ref, cell_ref, centre_ref, height_ref, spec_ref, left_ref, pair_ref, *rest
):
    pieces, (out_ref, held, sems) = rest[:8], rest[8:]

    def fetch(tile, carry):
        set_id = class_ref[tile]
        first = (place_ref[0] - (set_id // place_ref[2])) & 3
        second = (place_ref[1] - (set_id // place_ref[3])) & 3
        which = second * 2 + first // 2
        for at, ref in enumerate(pieces):

            @pl.when(which == at)
            def _():
                pltpu.make_async_copy(ref.at[first & 1], held.at[tile], sems.at[tile]).start()

        return carry

    lax.fori_loop(0, TILES, fetch, 0)
    heights = height_ref[...]
    mean = jnp.sum(heights, keepdims=True) * (1.0 / (SC * SC))
    height_row = lax.broadcasted_iota(jnp.int32, heights.shape, 0)
    height_lane = lax.broadcasted_iota(jnp.int32, heights.shape, 1)

    def some_tiles(trip, carry):
        batch = [trip * 2, trip * 2 + 1]
        for t in batch:
            pltpu.make_async_copy(pieces[0].at[0], held.at[t], sems.at[t]).wait()
        for t in batch:
            cell = cell_ref[t]
            row = cell // SC
            here = (height_row == (row & 7)) & (height_lane == (row // 8) * SC + (cell & (SC - 1)))
            shift = jnp.sum(jnp.where(here, heights, 0.0), keepdims=True) - mean
            shift = GAIN_SCALE * shift - centre_ref[class_ref[t]]
            re_part = spec_ref[t, 0].astype(F32)
            im_part = spec_ref[t, 1].astype(F32)
            re_part = jnp.concatenate([re_part, re_part], axis=1)
            im_part = jnp.concatenate([im_part, im_part], axis=1)
            filtered = []
            for g in range(GROUPS):
                kern_re = held[t, g, 0].astype(F32) + shift * held[t, g, 2].astype(F32)
                kern_im = held[t, g, 1].astype(F32) + shift * held[t, g, 3].astype(F32)
                prod_re = kern_re * re_part - kern_im * im_part
                prod_im = kern_re * im_part + kern_im * re_part
                filtered.append(jnp.concatenate([prod_re.astype(BF16), prod_im.astype(BF16)], axis=0))
            along = jnp.dot(
                left_ref[...], jnp.concatenate(filtered, axis=1), preferred_element_type=F32
            ).astype(BF16)
            both = [
                jnp.concatenate([along[:Q, at : at + 2 * NF], along[Q:, at : at + 2 * NF]], axis=1)
                for at in range(0, GROUPS * 4 * NF, 2 * NF)
            ]
            fields = jnp.dot(jnp.concatenate(both, axis=0), pair_ref[...], preferred_element_type=F32)
            total = jnp.zeros((Q, Q), F32)
            for part in range(4):
                for at in range(0, GROUPS * 2 * Q, Q):
                    block = fields[at : at + Q, part * Q : (part + 1) * Q]
                    total = total + block * block
            out_ref[t] = total.astype(out_ref.dtype)
        return carry

    lax.fori_loop(0, TILES // 2, some_tiles, 0)


def image(place, classes, cells, centre, heights, spectra, pieces, dtype):
    return pl.pallas_call(
        image_kernel,
        in_specs=[SMEM] * 4 + [VMEM] * 4 + [ANY] * 8,
        out_specs=VMEM,
        out_shape=jax.ShapeDtypeStruct((TILES, Q, Q), dtype),
        scratch_shapes=[
            pltpu.VMEM((TILES, GROUPS, 4, NF, 4 * NF), BF16),
            pltpu.SemaphoreType.DMA((TILES,)),
        ],
        name="image",
        cost_estimate=pl.CostEstimate(flops=3 * 10**9, bytes_accessed=4 * 10**6, transcendentals=0),
    )(place, classes, cells, centre, heights, spectra, as_bf16(left_table()), as_bf16(pair_table()), *pieces)


def resist_kernel(count, own_ref, other_ref, resist_ref, resist_t_ref, out_ref):
    intensity = (own_ref[...] + other_ref[...].astype(F32)) * (1.0 / KER)
    intensity = intensity.astype(BF16).reshape(count * Q, Q)
    half_way = jnp.dot(intensity, resist_t_ref[...], preferred_element_type=F32).astype(BF16)
    for t in range(count):
        out_ref[t] = jnp.dot(
            resist_ref[...], half_way[t * Q : (t + 1) * Q], preferred_element_type=F32
        ).astype(BF16)


def resist(own, other, count=4):
    table = resist_table(P_SIZE, Q)
    return pl.pallas_call(
        functools.partial(resist_kernel, count),
        grid=(TILES // count,),
        in_specs=[tiles(count, Q, Q), tiles(count, Q, Q), fixed(P_SIZE, Q), fixed(Q, P_SIZE)],
        out_specs=tiles(count, P_SIZE, P_SIZE),
        out_shape=jax.ShapeDtypeStruct((TILES, P_SIZE, P_SIZE), BF16),
        name="resist",
        cost_estimate=pl.CostEstimate(flops=10**9, bytes_accessed=5 * 10**6, transcendentals=0),
    )(own, other, as_bf16(table), as_bf16(table.T))


PLACES = [(z, core, x, y) for z in range(4) for core in range(2) for x in range(4) for y in range(4)]


def place_of(z, core, x, y):
    return ((z * 2 + core) * 4 + x % 4) * 4 + y % 4


def ring(phase, step):
    pairs = []
    for z, core, x, y in PLACES:
        along_y = (core + phase) % 2 == 0
        to = (z, core, x, y + step) if along_y else (z, core, x + step, y)
        pairs.append((place_of(z, core, x, y), place_of(*to)))
    return pairs


def send(value, phase, step):
    return lax.ppermute(value, ALL, ring(phase, step))


def after_all(value, *others):
    return lax.optimization_barrier((value, *others))[0]


def partner(x):
    return lax.ppermute(x, "tile", [(t, t ^ 1) for t in range(8)])


def summed(x, axis):
    size = lax.axis_size(axis)
    copies = jnp.broadcast_to(x[None], (size, *x.shape))
    return jnp.sum(lax.all_to_all(copies, axis, 0, 0, tiled=True), axis=0)


def device_steps(mask_tiles, class_of_tile, cell_of_tile, kernels, class_center):
    core = lax.axis_index("tile") % 2
    focus = lax.axis_index("focus")
    x, y = focus // 4, focus % 4
    place = jnp.stack(
        [
            jnp.where(core == 0, y, x),
            jnp.where(core == 0, x, y),
            jnp.where(core == 0, 1, 4),
            jnp.where(core == 0, 4, 1),
        ]
    ).astype(jnp.int32)
    classes = class_of_tile[:, 0]
    other_labels = partner(jnp.concatenate([classes, cell_of_tile]))

    mine = lax.dynamic_slice_in_dim(kernels[0], core * HALF, HALF, 0)
    mine = mine.reshape(GROUPS, 4, 4, NF, NF).transpose(0, 2, 3, 1, 4).reshape(GROUPS, 4, NF, 4 * NF)
    before = send(mine, 0, 1)
    after = send(mine, 0, -1)
    far = send(mine, 0, 2)
    spectra, heights = analyse(mask_tiles, cell_of_tile)
    low = jnp.stack([mine, after_all(before, heights)])
    high = jnp.stack([after_all(far, heights), after])
    low_before = send(low, 1, 1)
    high_after = send(high, 1, -1)
    high_before = send(high, 1, 1)
    low_after = send(low, 1, -1)
    heights = summed(heights, "tile")
    low_far = send(after_all(low_before, heights), 1, 1)
    high_far = send(after_all(high_after, heights), 1, -1)
    heights = summed(heights, "focus")
    other_spectra = partner(spectra)
    pieces = (low, high, low_before, high_before, low_far, high_far, low_after, high_after)
    other = image(
        place, other_labels[:TILES], other_labels[TILES:], class_center, heights, other_spectra, pieces, BF16
    )
    other = partner(other)
    own = image(place, classes, cell_of_tile, class_center, heights, spectra, pieces, F32)
    return resist(own, other)


def solution(mesh):
    placed = (
        P(("tile", "focus"), None, None),
        P(("tile", "focus"), None),
        P(("tile", "focus")),
        P("focus", None, None, None),
        P(),
    )
    return jax.shard_map(
        device_steps,
        mesh=mesh,
        in_specs=placed,
        out_specs=P(("tile", "focus"), None, None),
        check_vma=False,
    )
```

```python
import jax
import jax.numpy as jnp
import numpy as np
from jax import lax
from jax.experimental import pallas as pl
from jax.experimental.pallas import tpu as pltpu
from jax.sharding import PartitionSpec as P


P_SIZE = 512
NF = 64
KER = 24
BLK_PX = 64
SC = 32
NSUP = 1024
Q = 128
B = 8
REACH = 64
GRID = SC * B
HALF = KER // 2
GROUPS = HALF // 4
TILES = 8
GAIN_SCALE = 50.0
ALL = ("tile", "focus")
BEST = lax.Precision.HIGHEST
F32 = jnp.float32
BF16 = jnp.bfloat16


def spectral_table(freq_count, length):
    frequency = np.arange(freq_count) - freq_count // 2
    phases = np.mod(frequency[:, None] * np.arange(length)[None, :], length) * (2.0 * np.pi / length)
    return np.cos(phases), np.sin(phases)


def wave_table():
    return np.concatenate(spectral_table(NF, P_SIZE), axis=0)


def left_table():
    c, s = spectral_table(NF, Q)
    return np.concatenate(
        [np.concatenate([c.T, -s.T], axis=1), np.concatenate([s.T, c.T], axis=1)], axis=0
    )


def pair_table():
    c, s = spectral_table(NF, Q)
    z = np.zeros((NF, 2 * Q))
    up = np.concatenate([c, s], axis=1)
    down = np.concatenate([-s, c], axis=1)
    return np.block([[up, z], [z, up], [down, z], [z, down]])


def resist_table(pixels, samples):
    cos_pix, sin_pix = spectral_table(samples, pixels)
    cos_smp, sin_smp = spectral_table(samples, samples)
    frequency = np.arange(samples) - samples // 2
    weight = np.exp(-0.5 * (frequency * (4.0 / samples)) ** 2)[:, None]
    return ((cos_pix * weight).T @ cos_smp + (sin_pix * weight).T @ sin_smp) / samples


def spread_table(extent, length):
    places = np.arange(extent)
    weight = np.exp(-np.abs(places[:, None] - places[None, :]) / length)
    return weight / np.sum(weight, axis=1, keepdims=True)


def height_tables():
    spread = spread_table(GRID, REACH)
    rows = spread.reshape(SC, B, SC, B).mean(axis=1)
    cols = spread.reshape(SC, B, SC, B).mean(axis=3)
    row_part = np.tile(rows.transpose(1, 2, 0), (1, 1, 4))
    col_part = np.tile(cols, (1, 1, 4)) / (BLK_PX * BLK_PX)
    return row_part.astype(np.float32), col_part.astype(np.float32)


def as_bf16(table):
    return jnp.asarray(table.astype(np.float32)).astype(BF16)


SMEM = pl.BlockSpec(memory_space=pltpu.SMEM)
VMEM = pl.BlockSpec(memory_space=pltpu.VMEM)
ANY = pl.BlockSpec(memory_space=pl.ANY)


def analyse_kernel(
    cell_ref, mask_hbm, wave_t_hbm, wave_hbm, row_hbm, col_hbm, spec_ref, height_ref,
    mask, wave_t_ref, wave_ref, row_ref, col_ref, rows, along, sems, table_sems,
):
    def copy(t):
        return pltpu.make_async_copy(mask_hbm.at[t], mask.at[t], sems.at[t])

    tables = [
        pltpu.make_async_copy(source, target, table_sems.at[at])
        for at, (source, target) in enumerate(
            ((row_hbm, row_ref), (col_hbm, col_ref), (wave_t_hbm, wave_t_ref), (wave_hbm, wave_ref))
        )
    ]
    for t in range(2):
        copy(t).start()
    for table in tables:
        table.start()
    for t in range(2, TILES):
        copy(t).start()
    for table in tables:
        table.wait()
    lower = lax.broadcasted_iota(jnp.int32, (NF, 2 * NF), 1) < NF
    left = lax.broadcasted_iota(jnp.int32, (B, 2 * BLK_PX), 1) < BLK_PX
    scale = 1.0 / P_SIZE

    def some_tiles(trip, carry):
        batch = [trip * 2, trip * 2 + 1]
        for t in batch:
            copy(t).wait()
        for t in batch:
            cell = cell_ref[t]
            at = pl.ds(pl.multiple_of(t * B, B), B)
            col = col_ref[cell & (SC - 1)]
            wide = mask[t].astype(F32)
            sums = jnp.sum((wide * wide).reshape(B, BLK_PX, P_SIZE), axis=1)
            spread = jnp.zeros((B, 4 * SC), F32)
            for pair in range(B // 2):
                two = sums[:, pair * 2 * BLK_PX : (pair + 1) * 2 * BLK_PX]
                first = jnp.sum(jnp.where(left, two, 0.0), axis=1, keepdims=True)
                second = jnp.sum(jnp.where(left, 0.0, two), axis=1, keepdims=True)
                spread = spread + first * col[2 * pair : 2 * pair + 1] + second * col[2 * pair + 1 : 2 * pair + 2]
            along[at, :] = spread
            rows[at, :] = row_ref[cell // SC]
        for t in batch:
            projected = jnp.dot(mask[t], wave_t_ref[...], preferred_element_type=F32).astype(BF16)
            raw = jnp.dot(wave_ref[...], projected, preferred_element_type=F32)
            turned = pltpu.roll(raw, NF, 1)
            re = (raw[:NF] - turned[NF:]) * scale
            im = (turned[:NF] + raw[NF:]) * (-scale)
            spec_ref[t, 0] = jnp.where(lower, re, pltpu.roll(re, NF, 1)).astype(BF16)
            spec_ref[t, 1] = jnp.where(lower, im, pltpu.roll(im, NF, 1)).astype(BF16)
        return carry

    lax.fori_loop(0, TILES // 2, some_tiles, 0)
    whole = lax.dot_general(
        rows[...], along[...], (((0,), (0,)), ((), ())), precision=BEST, preferred_element_type=F32
    )
    quarter = lax.broadcasted_iota(jnp.int32, (B, 4 * SC), 1) // SC
    part = jnp.zeros((B, 4 * SC), F32)
    for q in range(4):
        part = jnp.where(quarter == q, whole[q * B : (q + 1) * B], part)
    height_ref[...] = part


def analyse(mask_tiles, cell_of_tile):
    wave = wave_table()
    row_part, col_part = height_tables()
    return pl.pallas_call(
        analyse_kernel,
        in_specs=[SMEM] + [ANY] * 5,
        out_specs=[VMEM, VMEM],
        out_shape=[
            jax.ShapeDtypeStruct((TILES, 2, NF, 2 * NF), BF16),
            jax.ShapeDtypeStruct((B, 4 * SC), F32),
        ],
        scratch_shapes=[
            pltpu.VMEM((TILES, P_SIZE, P_SIZE), BF16),
            pltpu.VMEM((P_SIZE, 2 * NF), BF16),
            pltpu.VMEM((2 * NF, P_SIZE), BF16),
            pltpu.VMEM((SC, B, 4 * SC), F32),
            pltpu.VMEM((SC, B, 4 * SC), F32),
            pltpu.VMEM((TILES * B, 4 * SC), F32),
            pltpu.VMEM((TILES * B, 4 * SC), F32),
            pltpu.SemaphoreType.DMA((TILES,)),
            pltpu.SemaphoreType.DMA((4,)),
        ],
        name="analyse",
        compiler_params=pltpu.CompilerParams(vmem_limit_bytes=12 << 20),
        cost_estimate=pl.CostEstimate(flops=10**9, bytes_accessed=6 * 10**6, transcendentals=0),
    )(cell_of_tile, mask_tiles, as_bf16(wave.T), as_bf16(wave), jnp.asarray(row_part), jnp.asarray(col_part))


def image_kernel(
    first_ref, second_ref, first_div_ref, second_div_ref, label_ref, centre_ref, height_ref,
    spec_hbm, left_hbm, pair_hbm, *rest
):
    pieces, (out_ref, held, spec_ref, left_ref, pair_ref, sems, table_sems) = rest[:8], rest[8:]
    tables = [
        pltpu.make_async_copy(source, target, table_sems.at[at])
        for at, (source, target) in enumerate(
            ((spec_hbm, spec_ref), (left_hbm, left_ref), (pair_hbm, pair_ref))
        )
    ]
    for table in tables:
        table.start()

    def fetch(tile, carry):
        set_id = label_ref[tile] // NSUP
        first = (first_ref[0] - (set_id // first_div_ref[0])) & 3
        second = (second_ref[0] - (set_id // second_div_ref[0])) & 3
        which = second * 2 + first // 2
        for at, ref in enumerate(pieces):

            @pl.when(which == at)
            def _():
                pltpu.make_async_copy(ref.at[first & 1], held.at[tile], sems.at[tile]).start()

        return carry

    lax.fori_loop(0, TILES, fetch, 0)
    heights = height_ref[...]
    mean = jnp.sum(heights, keepdims=True) * (1.0 / (SC * SC))
    height_row = lax.broadcasted_iota(jnp.int32, heights.shape, 0)
    height_lane = lax.broadcasted_iota(jnp.int32, heights.shape, 1)

    for table in tables:
        table.wait()

    def some_tiles(trip, carry):
        batch = [trip * 4 + at for at in range(4)]
        for t in batch:
            pltpu.make_async_copy(pieces[0].at[0], held.at[t], sems.at[t]).wait()
        for t in batch:
            cell = label_ref[t] & (NSUP - 1)
            row = cell // SC
            here = (height_row == (row & 7)) & (height_lane == (row // 8) * SC + (cell & (SC - 1)))
            shift = jnp.sum(jnp.where(here, heights, 0.0), keepdims=True) - mean
            shift = GAIN_SCALE * shift - centre_ref[label_ref[t] // NSUP]
            re_part = spec_ref[t, 0].astype(F32)
            im_part = spec_ref[t, 1].astype(F32)
            re_part = jnp.concatenate([re_part, re_part], axis=1)
            im_part = jnp.concatenate([im_part, im_part], axis=1)
            filtered = []
            for g in range(GROUPS):
                kern_re = held[t, g, 0].astype(F32) + shift * held[t, g, 2].astype(F32)
                kern_im = held[t, g, 1].astype(F32) + shift * held[t, g, 3].astype(F32)
                prod_re = kern_re * re_part - kern_im * im_part
                prod_im = kern_re * im_part + kern_im * re_part
                filtered.append(jnp.concatenate([prod_re.astype(BF16), prod_im.astype(BF16)], axis=0))
            along = jnp.dot(
                left_ref[...], jnp.concatenate(filtered, axis=1), preferred_element_type=F32
            ).astype(BF16)
            for rows in range(0, Q, Q // 2):
                both = [
                    jnp.concatenate(
                        [along[rows + half : rows + half + Q // 2, at : at + 2 * NF] for half in (0, Q)],
                        axis=1,
                    )
                    for at in range(0, GROUPS * 4 * NF, 2 * NF)
                ]
                fields = jnp.dot(jnp.concatenate(both, axis=0), pair_ref[...], preferred_element_type=F32)
                total = jnp.zeros((Q // 2, Q), F32)
                for at in range(0, GROUPS * Q, Q // 2):
                    for part in range(4):
                        block = fields[at : at + Q // 2, part * Q : (part + 1) * Q]
                        total = total + block * block
                out_ref[t, rows : rows + Q // 2] = total.astype(out_ref.dtype)
        return carry

    lax.fori_loop(0, TILES // 4, some_tiles, 0)


def image(place, labels, centre, heights, spectra, pieces):
    return pl.pallas_call(
        image_kernel,
        in_specs=[SMEM] * 6 + [VMEM] + [ANY] * 11,
        out_specs=VMEM,
        out_shape=jax.ShapeDtypeStruct((TILES, Q, Q), BF16),
        scratch_shapes=[
            pltpu.VMEM((TILES, GROUPS, 4, NF, 4 * NF), BF16),
            pltpu.VMEM((TILES, 2, NF, 2 * NF), BF16),
            pltpu.VMEM((2 * Q, 2 * NF), BF16),
            pltpu.VMEM((4 * NF, 4 * Q), BF16),
            pltpu.SemaphoreType.DMA((TILES,)),
            pltpu.SemaphoreType.DMA((3,)),
        ],
        name="image",
        compiler_params=pltpu.CompilerParams(vmem_limit_bytes=16 << 20),
        cost_estimate=pl.CostEstimate(flops=3 * 10**9, bytes_accessed=4 * 10**6, transcendentals=0),
    )(*place, labels, centre, heights, spectra, as_bf16(left_table()), as_bf16(pair_table()), *pieces)


def resist_kernel(
    own_hbm, other_hbm, resist_hbm, resist_t_hbm, out_hbm,
    own_ref, other_ref, resist_ref, resist_t_ref, image_ref, sems, out_sems,
):
    copies = [
        pltpu.make_async_copy(source, target, sems.at[at])
        for at, (source, target) in enumerate(
            (
                (own_hbm, own_ref),
                (other_hbm, other_ref),
                (resist_t_hbm, resist_t_ref),
                (resist_hbm, resist_ref),
            )
        )
    ]
    for copy in copies:
        copy.start()
    for copy in copies:
        copy.wait()

    def some_tiles(trip, carry):
        at = pl.ds(trip * 2, 2)
        intensity = (own_ref[at].astype(F32) + other_ref[at].astype(F32)) * (1.0 / KER)
        intensity = intensity.astype(BF16).reshape(2 * Q, Q)
        half_way = jnp.dot(intensity, resist_t_ref[...], preferred_element_type=F32).astype(BF16)
        for t in range(2):
            image_ref[trip * 2 + t] = jnp.dot(
                resist_ref[...], half_way[t * Q : (t + 1) * Q], preferred_element_type=F32
            ).astype(BF16)
            out_copy(trip * 2 + t).start()
        return carry

    def out_copy(t):
        return pltpu.make_async_copy(image_ref.at[t], out_hbm.at[t], out_sems.at[t])

    lax.fori_loop(0, TILES // 2, some_tiles, 0)
    for t in range(TILES):
        out_copy(t).wait()


def resist(own, other):
    table = resist_table(P_SIZE, Q)
    return pl.pallas_call(
        resist_kernel,
        in_specs=[ANY] * 4,
        out_specs=ANY,
        out_shape=jax.ShapeDtypeStruct((TILES, P_SIZE, P_SIZE), BF16),
        scratch_shapes=[
            pltpu.VMEM((TILES, Q, Q), BF16),
            pltpu.VMEM((TILES, Q, Q), BF16),
            pltpu.VMEM((P_SIZE, Q), BF16),
            pltpu.VMEM((Q, P_SIZE), BF16),
            pltpu.VMEM((TILES, P_SIZE, P_SIZE), BF16),
            pltpu.SemaphoreType.DMA((4,)),
            pltpu.SemaphoreType.DMA((TILES,)),
        ],
        name="resist",
        compiler_params=pltpu.CompilerParams(vmem_limit_bytes=12 << 20),
        cost_estimate=pl.CostEstimate(flops=10**9, bytes_accessed=5 * 10**6, transcendentals=0),
    )(own, other, as_bf16(table), as_bf16(table.T))


PLACES = [(z, core, x, y) for z in range(4) for core in range(2) for x in range(4) for y in range(4)]


def place_of(z, core, x, y):
    return ((z * 2 + core) * 4 + x % 4) * 4 + y % 4


def ring(phase, step):
    pairs = []
    for z, core, x, y in PLACES:
        along_y = (core + phase) % 2 == 0
        to = (z, core, x, y + step) if along_y else (z, core, x + step, y)
        pairs.append((place_of(z, core, x, y), place_of(*to)))
    return pairs


def send(value, phase, step):
    return lax.ppermute(value, ALL, ring(phase, step))


def after_all(value, *others):
    return lax.optimization_barrier((value, *others))[0]


def partner(x):
    return lax.ppermute(x, "tile", [(t, t ^ 1) for t in range(8)])


def summed(x, axis):
    size = lax.axis_size(axis)
    copies = jnp.broadcast_to(x[None], (size, *x.shape))
    return jnp.sum(lax.all_to_all(copies, axis, 0, 0, tiled=True), axis=0)


def device_steps(mask_tiles, class_of_tile, cell_of_tile, kernels, class_center):
    core = lax.axis_index("tile") % 2
    focus = lax.axis_index("focus")
    x, y = focus // 4, focus % 4
    place = [
        jnp.reshape(value.astype(jnp.int32), (1,))
        for value in (
            jnp.where(core == 0, y, x),
            jnp.where(core == 0, x, y),
            jnp.where(core == 0, 1, 4),
            jnp.where(core == 0, 4, 1),
        )
    ]
    labels = class_of_tile[:, 0] * NSUP + cell_of_tile
    other_labels = partner(labels)

    mine = lax.dynamic_slice_in_dim(kernels[0], core * HALF, HALF, 0)
    mine = mine.reshape(GROUPS, 4, 4, NF, NF).transpose(0, 2, 3, 1, 4).reshape(GROUPS, 4, NF, 4 * NF)
    before = send(mine, 0, 1)
    after = send(mine, 0, -1)
    far = send(mine, 0, 2)
    spectra, heights = analyse(mask_tiles, cell_of_tile)
    low = jnp.stack([mine, after_all(before, heights)])
    high = jnp.stack([after_all(far, heights), after])
    low_before = send(low, 1, 1)
    high_after = send(high, 1, -1)
    high_before = send(high, 1, 1)
    low_after = send(low, 1, -1)
    heights = summed(heights, "tile")
    low_far = send(after_all(low_before, heights), 1, 1)
    high_far = send(after_all(high_after, heights), 1, -1)
    heights = summed(heights, "focus")
    other_spectra = partner(spectra)
    pieces = (low, high, low_before, high_before, low_far, high_far, low_after, high_after)
    other = image(place, other_labels, class_center, heights, other_spectra, pieces)
    other = partner(other)
    own = image(place, labels, class_center, heights, spectra, pieces)
    return resist(own, other)


def solution(mesh):
    placed = (
        P(("tile", "focus"), None, None),
        P(("tile", "focus"), None),
        P(("tile", "focus")),
        P("focus", None, None, None),
        P(),
    )
    return jax.shard_map(
        device_steps,
        mesh=mesh,
        in_specs=placed,
        out_specs=P(("tile", "focus"), None, None),
        check_vma=False,
    )
```

```python
import functools

import jax
import jax.numpy as jnp
import numpy as np
from jax import lax
from jax.experimental import pallas as pl
from jax.experimental.pallas import tpu as pltpu
from jax.sharding import PartitionSpec as P


P_SIZE = 512
NF = 64
KER = 24
BLK_PX = 64
SC = 32
NSUP = 1024
Q = 128
B = 8
REACH = 64
GRID = SC * B
HALF = KER // 2
GROUPS = HALF // 4
TILES = 8
GAIN_SCALE = 50.0
ALL = ("tile", "focus")
BEST = lax.Precision.HIGHEST
F32 = jnp.float32
BF16 = jnp.bfloat16


def spectral_table(freq_count, length):
    frequency = np.arange(freq_count) - freq_count // 2
    phases = np.mod(frequency[:, None] * np.arange(length)[None, :], length) * (2.0 * np.pi / length)
    return np.cos(phases), np.sin(phases)


def wave_table():
    return np.concatenate(spectral_table(NF, P_SIZE), axis=0)


def left_table():
    c, s = spectral_table(NF, Q)
    return np.concatenate(
        [np.concatenate([c.T, -s.T], axis=1), np.concatenate([s.T, c.T], axis=1)], axis=0
    )


def image_table():
    c, s = spectral_table(NF, Q)
    return np.concatenate([np.concatenate([c, s], axis=1), np.concatenate([-s, c], axis=1)], axis=0)


def resist_table(pixels, samples):
    cos_pix, sin_pix = spectral_table(samples, pixels)
    cos_smp, sin_smp = spectral_table(samples, samples)
    frequency = np.arange(samples) - samples // 2
    weight = np.exp(-0.5 * (frequency * (4.0 / samples)) ** 2)[:, None]
    return ((cos_pix * weight).T @ cos_smp + (sin_pix * weight).T @ sin_smp) / samples


def spread_table(extent, length):
    places = np.arange(extent)
    weight = np.exp(-np.abs(places[:, None] - places[None, :]) / length)
    return weight / np.sum(weight, axis=1, keepdims=True)


def height_tables():
    spread = spread_table(GRID, REACH)
    rows = spread.reshape(SC, B, SC, B).mean(axis=1)
    cols = spread.reshape(SC, B, SC, B).mean(axis=3)
    row_part = np.tile(rows.transpose(1, 2, 0), (1, 1, 4))
    col_part = np.tile(cols, (1, 1, 4)) / (BLK_PX * BLK_PX)
    return row_part.astype(np.float32), col_part.astype(np.float32)


def as_bf16(table):
    return jnp.asarray(table.astype(np.float32)).astype(BF16)


SMEM = pl.BlockSpec(memory_space=pltpu.SMEM)
VMEM = pl.BlockSpec(memory_space=pltpu.VMEM)
ANY = pl.BlockSpec(memory_space=pl.ANY)
HBM = pl.BlockSpec(memory_space=pltpu.HBM)


def density_kernel(cell_ref, mask_hbm, row_hbm, col_hbm, height_ref, mask, row_ref, col_ref, rows, along, sems, table_sems):
    def copy(t):
        return pltpu.make_async_copy(mask_hbm.at[t], mask.at[t], sems.at[t])

    tables = [
        pltpu.make_async_copy(row_hbm, row_ref, table_sems.at[0]),
        pltpu.make_async_copy(col_hbm, col_ref, table_sems.at[1]),
    ]
    for t in range(2):
        copy(t).start()
    for table in tables:
        table.start()
    for t in range(2, TILES):
        copy(t).start()
    left = lax.broadcasted_iota(jnp.int32, (B, 2 * BLK_PX), 1) < BLK_PX
    for table in tables:
        table.wait()

    def some_tiles(trip, carry):
        batch = [trip * 2, trip * 2 + 1]
        for t in batch:
            copy(t).wait()
        for t in batch:
            cell = cell_ref[t]
            at = pl.ds(pl.multiple_of(t * B, B), B)
            col = col_ref[cell & (SC - 1)]
            wide = mask[t].astype(F32)
            sums = jnp.sum((wide * wide).reshape(B, BLK_PX, P_SIZE), axis=1)
            spread = jnp.zeros((B, 4 * SC), F32)
            for pair in range(B // 2):
                two = sums[:, pair * 2 * BLK_PX : (pair + 1) * 2 * BLK_PX]
                first = jnp.sum(jnp.where(left, two, 0.0), axis=1, keepdims=True)
                second = jnp.sum(jnp.where(left, 0.0, two), axis=1, keepdims=True)
                spread = spread + first * col[2 * pair : 2 * pair + 1] + second * col[2 * pair + 1 : 2 * pair + 2]
            along[at, :] = spread
            rows[at, :] = row_ref[cell // SC]
        return carry

    lax.fori_loop(0, TILES // 2, some_tiles, 0)
    whole = lax.dot_general(
        rows[...], along[...], (((0,), (0,)), ((), ())), precision=BEST, preferred_element_type=F32
    )
    quarter = lax.broadcasted_iota(jnp.int32, (B, 4 * SC), 1) // SC
    part = jnp.zeros((B, 4 * SC), F32)
    for q in range(4):
        part = jnp.where(quarter == q, whole[q * B : (q + 1) * B], part)
    height_ref[...] = part


def density_heights(mask_tiles, cell_of_tile):
    row_part, col_part = height_tables()
    return pl.pallas_call(
        density_kernel,
        in_specs=[SMEM] + [HBM] * 3,
        out_specs=VMEM,
        out_shape=jax.ShapeDtypeStruct((B, 4 * SC), F32),
        scratch_shapes=[
            pltpu.VMEM((TILES, P_SIZE, P_SIZE), BF16),
            pltpu.VMEM((SC, B, 4 * SC), F32),
            pltpu.VMEM((SC, B, 4 * SC), F32),
            pltpu.VMEM((TILES * B, 4 * SC), F32),
            pltpu.VMEM((TILES * B, 4 * SC), F32),
            pltpu.SemaphoreType.DMA((TILES,)),
            pltpu.SemaphoreType.DMA((2,)),
        ],
        name="density",
        cost_estimate=pl.CostEstimate(flops=10**7, bytes_accessed=5 * 10**6, transcendentals=0),
    )(cell_of_tile, mask_tiles, jnp.asarray(row_part), jnp.asarray(col_part))


def spectra_kernel(step, mask_hbm, wave_t_hbm, wave_hbm, spec_ref, mask, wave_t_ref, wave_ref, sems, table_sems):
    def copy(t):
        return pltpu.make_async_copy(mask_hbm.at[t], mask.at[t], sems.at[t])

    tables = [
        pltpu.make_async_copy(wave_t_hbm, wave_t_ref, table_sems.at[0]),
        pltpu.make_async_copy(wave_hbm, wave_ref, table_sems.at[1]),
    ]
    for table in tables:
        table.start()
    for t in range(TILES):
        copy(t).start()
    lower = lax.broadcasted_iota(jnp.int32, (NF, 2 * NF), 1) < NF
    scale = 1.0 / P_SIZE
    for table in tables:
        table.wait()

    def some_tiles(trip, carry):
        batch = [trip * step + at for at in range(step)]
        for t in batch:
            copy(t).wait()
        every = mask[pl.ds(trip * step, step)].reshape(step * P_SIZE, P_SIZE)
        projected = jnp.dot(every, wave_t_ref[...], preferred_element_type=F32).astype(BF16)
        for at, t in enumerate(batch):
            raw = jnp.dot(
                wave_ref[...], projected[at * P_SIZE : (at + 1) * P_SIZE], preferred_element_type=F32
            )
            turned = pltpu.roll(raw, NF, 1)
            re = (raw[:NF] - turned[NF:]) * scale
            im = (turned[:NF] + raw[NF:]) * (-scale)
            spec_ref[t, 0] = jnp.where(lower, re, pltpu.roll(re, NF, 1)).astype(BF16)
            spec_ref[t, 1] = jnp.where(lower, im, pltpu.roll(im, NF, 1)).astype(BF16)
        return carry

    lax.fori_loop(0, TILES // step, some_tiles, 0)


def form_spectra(mask_tiles, step=4):
    wave = wave_table()
    return pl.pallas_call(
        functools.partial(spectra_kernel, step),
        in_specs=[HBM] * 3,
        out_specs=VMEM,
        out_shape=jax.ShapeDtypeStruct((TILES, 2, NF, 2 * NF), BF16),
        scratch_shapes=[
            pltpu.VMEM((TILES, P_SIZE, P_SIZE), BF16),
            pltpu.VMEM((P_SIZE, 2 * NF), BF16),
            pltpu.VMEM((2 * NF, P_SIZE), BF16),
            pltpu.SemaphoreType.DMA((TILES,)),
            pltpu.SemaphoreType.DMA((2,)),
        ],
        name="spectra",
        cost_estimate=pl.CostEstimate(flops=10**9, bytes_accessed=5 * 10**6, transcendentals=0),
    )(mask_tiles, as_bf16(wave.T), as_bf16(wave))


def image_kernel(
    first_ref, second_ref, first_div_ref, second_div_ref, label_ref, centre_ref, height_ref,
    spec_hbm, left_hbm, right_hbm, *rest
):
    pieces, (out_ref, held, spec_ref, left_ref, right_ref, pair_ref, sems, table_sems) = rest[:8], rest[8:]
    tables = [
        pltpu.make_async_copy(source, target, table_sems.at[at])
        for at, (source, target) in enumerate(
            ((right_hbm, right_ref), (left_hbm, left_ref), (spec_hbm, spec_ref))
        )
    ]
    for table in tables:
        table.start()

    def fetch(tile, carry):
        set_id = label_ref[tile] // NSUP
        first = (first_ref[0] - (set_id // first_div_ref[0])) & 3
        second = (second_ref[0] - (set_id // second_div_ref[0])) & 3
        which = second * 2 + first // 2
        for at, ref in enumerate(pieces):

            @pl.when(which == at)
            def _():
                pltpu.make_async_copy(ref.at[first & 1], held.at[tile], sems.at[tile]).start()

        return carry

    lax.fori_loop(0, TILES, fetch, 0)
    heights = height_ref[...]
    mean = jnp.sum(heights, keepdims=True) * (1.0 / (SC * SC))
    height_row = lax.broadcasted_iota(jnp.int32, heights.shape, 0)
    height_lane = lax.broadcasted_iota(jnp.int32, heights.shape, 1)

    for table in tables:
        table.wait()
    for at in range(4):
        rows = slice(at * NF, (at + 1) * NF)
        block = right_ref[(at // 2) * NF : (at // 2 + 1) * NF]
        pair_ref[rows, (at % 2) * 2 * Q : (at % 2 + 1) * 2 * Q] = block
        pair_ref[rows, (1 - at % 2) * 2 * Q : (2 - at % 2) * 2 * Q] = jnp.zeros_like(block)

    def some_tiles(trip, carry):
        batch = [trip * 4 + at for at in range(4)]
        for t in batch:
            pltpu.make_async_copy(pieces[0].at[0], held.at[t], sems.at[t]).wait()
        for t in batch:
            cell = label_ref[t] & (NSUP - 1)
            row = cell // SC
            here = (height_row == (row & 7)) & (height_lane == (row // 8) * SC + (cell & (SC - 1)))
            shift = jnp.sum(jnp.where(here, heights, 0.0), keepdims=True) - mean
            shift = GAIN_SCALE * shift - centre_ref[label_ref[t] // NSUP]
            re_part = spec_ref[t, 0].astype(F32)
            im_part = spec_ref[t, 1].astype(F32)
            re_part = jnp.concatenate([re_part, re_part], axis=1)
            im_part = jnp.concatenate([im_part, im_part], axis=1)
            filtered = []
            for g in range(GROUPS):
                kern_re = held[t, g, 0].astype(F32) + shift * held[t, g, 2].astype(F32)
                kern_im = held[t, g, 1].astype(F32) + shift * held[t, g, 3].astype(F32)
                prod_re = kern_re * re_part - kern_im * im_part
                prod_im = kern_re * im_part + kern_im * re_part
                filtered.append(jnp.concatenate([prod_re.astype(BF16), prod_im.astype(BF16)], axis=0))
            along = jnp.dot(
                left_ref[...], jnp.concatenate(filtered, axis=1), preferred_element_type=F32
            ).astype(BF16)
            for rows in range(0, Q, Q // 2):
                both = [
                    jnp.concatenate(
                        [along[rows + half : rows + half + Q // 2, at : at + 2 * NF] for half in (0, Q)],
                        axis=1,
                    )
                    for at in range(0, GROUPS * 4 * NF, 2 * NF)
                ]
                fields = jnp.dot(jnp.concatenate(both, axis=0), pair_ref[...], preferred_element_type=F32)
                total = jnp.zeros((Q // 2, Q), F32)
                for at in range(0, GROUPS * Q, Q // 2):
                    for part in range(4):
                        block = fields[at : at + Q // 2, part * Q : (part + 1) * Q]
                        total = total + block * block
                out_ref[t, rows : rows + Q // 2] = total.astype(out_ref.dtype)
        return carry

    lax.fori_loop(0, TILES // 4, some_tiles, 0)


def image(place, labels, centre, heights, spectra, pieces):
    return pl.pallas_call(
        image_kernel,
        in_specs=[SMEM] * 6 + [VMEM, ANY, HBM, HBM] + [ANY] * 8,
        out_specs=VMEM,
        out_shape=jax.ShapeDtypeStruct((TILES, Q, Q), BF16),
        scratch_shapes=[
            pltpu.VMEM((TILES, GROUPS, 4, NF, 4 * NF), BF16),
            pltpu.VMEM((TILES, 2, NF, 2 * NF), BF16),
            pltpu.VMEM((2 * Q, 2 * NF), BF16),
            pltpu.VMEM((2 * NF, 2 * Q), BF16),
            pltpu.VMEM((4 * NF, 4 * Q), BF16),
            pltpu.SemaphoreType.DMA((TILES,)),
            pltpu.SemaphoreType.DMA((3,)),
        ],
        name="image",
        compiler_params=pltpu.CompilerParams(vmem_limit_bytes=16 << 20),
        cost_estimate=pl.CostEstimate(flops=3 * 10**9, bytes_accessed=4 * 10**6, transcendentals=0),
    )(*place, labels, centre, heights, spectra, as_bf16(left_table()), as_bf16(image_table()), *pieces)


def resist_kernel(
    own_hbm, other_hbm, resist_hbm, resist_t_hbm, out_hbm,
    own_ref, other_ref, resist_ref, resist_t_ref, image_ref, sems, out_sems,
):
    copies = [
        pltpu.make_async_copy(source, target, sems.at[at])
        for at, (source, target) in enumerate(
            (
                (own_hbm, own_ref),
                (other_hbm, other_ref),
                (resist_t_hbm, resist_t_ref),
                (resist_hbm, resist_ref),
            )
        )
    ]
    for copy in copies:
        copy.start()
    for copy in copies:
        copy.wait()

    def some_tiles(trip, carry):
        at = pl.ds(trip * 2, 2)
        intensity = (own_ref[at].astype(F32) + other_ref[at].astype(F32)) * (1.0 / KER)
        intensity = intensity.astype(BF16).reshape(2 * Q, Q)
        half_way = jnp.dot(intensity, resist_t_ref[...], preferred_element_type=F32).astype(BF16)
        for t in range(2):
            image_ref[trip * 2 + t] = jnp.dot(
                resist_ref[...], half_way[t * Q : (t + 1) * Q], preferred_element_type=F32
            ).astype(BF16)
            out_copy(trip * 2 + t).start()
        return carry

    def out_copy(t):
        return pltpu.make_async_copy(image_ref.at[t], out_hbm.at[t], out_sems.at[t])

    lax.fori_loop(0, TILES // 2, some_tiles, 0)
    for t in range(TILES):
        out_copy(t).wait()


def resist(own, other):
    table = resist_table(P_SIZE, Q)
    return pl.pallas_call(
        resist_kernel,
        in_specs=[ANY, ANY, HBM, HBM],
        out_specs=ANY,
        out_shape=jax.ShapeDtypeStruct((TILES, P_SIZE, P_SIZE), BF16),
        scratch_shapes=[
            pltpu.VMEM((TILES, Q, Q), BF16),
            pltpu.VMEM((TILES, Q, Q), BF16),
            pltpu.VMEM((P_SIZE, Q), BF16),
            pltpu.VMEM((Q, P_SIZE), BF16),
            pltpu.VMEM((TILES, P_SIZE, P_SIZE), BF16),
            pltpu.SemaphoreType.DMA((4,)),
            pltpu.SemaphoreType.DMA((TILES,)),
        ],
        name="resist",
        compiler_params=pltpu.CompilerParams(vmem_limit_bytes=12 << 20),
        cost_estimate=pl.CostEstimate(flops=10**9, bytes_accessed=5 * 10**6, transcendentals=0),
    )(own, other, as_bf16(table), as_bf16(table.T))


PLACES = [(z, core, x, y) for z in range(4) for core in range(2) for x in range(4) for y in range(4)]


def place_of(z, core, x, y):
    return ((z * 2 + core) * 4 + x % 4) * 4 + y % 4


def ring(phase, step):
    pairs = []
    for z, core, x, y in PLACES:
        along_y = (core + phase) % 2 == 0
        to = (z, core, x, y + step) if along_y else (z, core, x + step, y)
        pairs.append((place_of(z, core, x, y), place_of(*to)))
    return pairs


def send(value, phase, step):
    return lax.ppermute(value, ALL, ring(phase, step))


def after_all(value, *others):
    return lax.optimization_barrier((value, *others))[0]


def partner(x):
    return lax.ppermute(x, "tile", [(t, t ^ 1) for t in range(8)])


def summed(x, axis):
    size = lax.axis_size(axis)
    copies = jnp.broadcast_to(x[None], (size, *x.shape))
    return jnp.sum(lax.all_to_all(copies, axis, 0, 0, tiled=True), axis=0)


def device_steps(mask_tiles, class_of_tile, cell_of_tile, kernels, class_center):
    core = lax.axis_index("tile") % 2
    focus = lax.axis_index("focus")
    x, y = focus // 4, focus % 4
    place = [
        jnp.reshape(value.astype(jnp.int32), (1,))
        for value in (
            jnp.where(core == 0, y, x),
            jnp.where(core == 0, x, y),
            jnp.where(core == 0, 1, 4),
            jnp.where(core == 0, 4, 1),
        )
    ]
    labels = class_of_tile[:, 0] * NSUP + cell_of_tile
    other_labels = partner(labels)

    mine = lax.dynamic_slice_in_dim(kernels[0], core * HALF, HALF, 0)
    mine = mine.reshape(GROUPS, 4, 4, NF, NF).transpose(0, 2, 3, 1, 4).reshape(GROUPS, 4, NF, 4 * NF)
    before = send(mine, 0, 1)
    after = send(mine, 0, -1)
    far = send(mine, 0, 2)
    heights = density_heights(mask_tiles, cell_of_tile)
    low = jnp.stack([mine, after_all(before, heights)])
    high = jnp.stack([after_all(far, heights), after])
    low_before = send(low, 1, 1)
    high_after = send(high, 1, -1)
    high_before = send(high, 1, 1)
    low_after = send(low, 1, -1)
    heights = summed(heights, "tile")
    spectra = form_spectra(mask_tiles)
    low_far = send(after_all(low_before, heights), 1, 1)
    high_far = send(after_all(high_after, heights), 1, -1)
    heights = summed(heights, "focus")
    other_spectra = partner(spectra)
    pieces = (low, high, low_before, high_before, low_far, high_far, low_after, high_after)
    other = image(place, other_labels, class_center, heights, other_spectra, pieces)
    other = partner(other)
    own = image(place, labels, class_center, heights, spectra, pieces)
    return resist(own, other)


def solution(mesh):
    placed = (
        P(("tile", "focus"), None, None),
        P(("tile", "focus"), None),
        P(("tile", "focus")),
        P("focus", None, None, None),
        P(),
    )
    return jax.shard_map(
        device_steps,
        mesh=mesh,
        in_specs=placed,
        out_specs=P(("tile", "focus"), None, None),
        check_vma=False,
    )
```

```python
import functools

import jax
import jax.numpy as jnp
import numpy as np
from jax import lax
from jax.experimental import pallas as pl
from jax.experimental.pallas import tpu as pltpu
from jax.sharding import PartitionSpec as P


P_SIZE = 512
NF = 64
KER = 24
BLK_PX = 64
SC = 32
NSUP = 1024
Q = 128
B = 8
REACH = 64
GRID = SC * B
HALF = KER // 2
GROUPS = HALF // 4
TILES = 8
GAIN_SCALE = 50.0
ALL = ("tile", "focus")
BEST = lax.Precision.HIGHEST
F32 = jnp.float32
BF16 = jnp.bfloat16


def spectral_table(freq_count, length):
    frequency = np.arange(freq_count) - freq_count // 2
    phases = np.mod(frequency[:, None] * np.arange(length)[None, :], length) * (2.0 * np.pi / length)
    return np.cos(phases), np.sin(phases)


def wave_table():
    return np.concatenate(spectral_table(NF, P_SIZE), axis=0)


def image_table():
    c, s = spectral_table(NF, Q)
    return np.concatenate([np.concatenate([c, s], axis=1), np.concatenate([-s, c], axis=1)], axis=0)


def resist_table(pixels, samples):
    cos_pix, sin_pix = spectral_table(samples, pixels)
    cos_smp, sin_smp = spectral_table(samples, samples)
    frequency = np.arange(samples) - samples // 2
    weight = np.exp(-0.5 * (frequency * (4.0 / samples)) ** 2)[:, None]
    return ((cos_pix * weight).T @ cos_smp + (sin_pix * weight).T @ sin_smp) / samples


def spread_table(extent, length):
    places = np.arange(extent)
    weight = np.exp(-np.abs(places[:, None] - places[None, :]) / length)
    return weight / np.sum(weight, axis=1, keepdims=True)


def height_tables():
    spread = spread_table(GRID, REACH)
    rows = spread.reshape(SC, B, SC, B).mean(axis=1)
    cols = spread.reshape(SC, B, SC, B).mean(axis=3)
    row_part = np.tile(rows.transpose(1, 2, 0), (1, 1, 4))
    col_part = np.tile(cols, (1, 1, 4)) / (BLK_PX * BLK_PX)
    return row_part.astype(np.float32), col_part.astype(np.float32)


def as_bf16(table):
    return jnp.asarray(table.astype(np.float32)).astype(BF16)


SMEM = pl.BlockSpec(memory_space=pltpu.SMEM)
VMEM = pl.BlockSpec(memory_space=pltpu.VMEM)
ANY = pl.BlockSpec(memory_space=pl.ANY)
HBM = pl.BlockSpec(memory_space=pltpu.HBM)


def density_kernel(cell_ref, mask_hbm, row_hbm, col_hbm, height_ref, mask, row_ref, col_ref, rows, along, sems, table_sems):
    def copy(t):
        return pltpu.make_async_copy(mask_hbm.at[t], mask.at[t], sems.at[t])

    tables = [
        pltpu.make_async_copy(row_hbm, row_ref, table_sems.at[0]),
        pltpu.make_async_copy(col_hbm, col_ref, table_sems.at[1]),
    ]
    for t in range(2):
        copy(t).start()
    for table in tables:
        table.start()
    for t in range(2, TILES):
        copy(t).start()
    left = lax.broadcasted_iota(jnp.int32, (B, 2 * BLK_PX), 1) < BLK_PX
    for table in tables:
        table.wait()

    def some_tiles(trip, carry):
        batch = [trip * 2, trip * 2 + 1]
        for t in batch:
            copy(t).wait()
        for t in batch:
            cell = cell_ref[t]
            at = pl.ds(pl.multiple_of(t * B, B), B)
            col = col_ref[cell & (SC - 1)]
            wide = mask[t].astype(F32)
            sums = jnp.sum((wide * wide).reshape(B, BLK_PX, P_SIZE), axis=1)
            spread = jnp.zeros((B, 4 * SC), F32)
            for pair in range(B // 2):
                two = sums[:, pair * 2 * BLK_PX : (pair + 1) * 2 * BLK_PX]
                first = jnp.sum(jnp.where(left, two, 0.0), axis=1, keepdims=True)
                second = jnp.sum(jnp.where(left, 0.0, two), axis=1, keepdims=True)
                spread = spread + first * col[2 * pair : 2 * pair + 1] + second * col[2 * pair + 1 : 2 * pair + 2]
            along[at, :] = spread
            rows[at, :] = row_ref[cell // SC]
        return carry

    lax.fori_loop(0, TILES // 2, some_tiles, 0)
    whole = lax.dot_general(
        rows[...], along[...], (((0,), (0,)), ((), ())), precision=BEST, preferred_element_type=F32
    )
    quarter = lax.broadcasted_iota(jnp.int32, (B, 4 * SC), 1) // SC
    part = jnp.zeros((B, 4 * SC), F32)
    for q in range(4):
        part = jnp.where(quarter == q, whole[q * B : (q + 1) * B], part)
    height_ref[...] = jnp.broadcast_to(part[None], height_ref.shape)


def density_heights(mask_tiles, cell_of_tile, copies):
    row_part, col_part = height_tables()
    return pl.pallas_call(
        density_kernel,
        in_specs=[SMEM] + [HBM] * 3,
        out_specs=VMEM,
        out_shape=jax.ShapeDtypeStruct((copies, B, 4 * SC), F32),
        scratch_shapes=[
            pltpu.VMEM((TILES, P_SIZE, P_SIZE), BF16),
            pltpu.VMEM((SC, B, 4 * SC), F32),
            pltpu.VMEM((SC, B, 4 * SC), F32),
            pltpu.VMEM((TILES * B, 4 * SC), F32),
            pltpu.VMEM((TILES * B, 4 * SC), F32),
            pltpu.SemaphoreType.DMA((TILES,)),
            pltpu.SemaphoreType.DMA((2,)),
        ],
        name="density",
        cost_estimate=pl.CostEstimate(flops=10**7, bytes_accessed=5 * 10**6, transcendentals=0),
    )(cell_of_tile, mask_tiles, jnp.asarray(row_part), jnp.asarray(col_part))


def spectra_kernel(step, mask_hbm, wave_t_hbm, wave_hbm, spec_ref, mask, wave_t_ref, wave_ref, sems, table_sems):
    def copy(t):
        return pltpu.make_async_copy(mask_hbm.at[t], mask.at[t], sems.at[t])

    tables = [
        pltpu.make_async_copy(wave_t_hbm, wave_t_ref, table_sems.at[0]),
        pltpu.make_async_copy(wave_hbm, wave_ref, table_sems.at[1]),
    ]
    for table in tables:
        table.start()
    for t in range(TILES):
        copy(t).start()
    lower = lax.broadcasted_iota(jnp.int32, (NF, 2 * NF), 1) < NF
    scale = 1.0 / P_SIZE
    for table in tables:
        table.wait()

    def some_tiles(trip, carry):
        batch = [trip * step + at for at in range(step)]
        for t in batch:
            copy(t).wait()
        every = mask[pl.ds(trip * step, step)].reshape(step * P_SIZE, P_SIZE)
        projected = jnp.dot(every, wave_t_ref[...], preferred_element_type=F32).astype(BF16)
        for at, t in enumerate(batch):
            raw = jnp.dot(
                wave_ref[...], projected[at * P_SIZE : (at + 1) * P_SIZE], preferred_element_type=F32
            )
            turned = pltpu.roll(raw, NF, 1)
            re = (raw[:NF] - turned[NF:]) * scale
            im = (turned[:NF] + raw[NF:]) * (-scale)
            spec_ref[t, 0] = jnp.where(lower, re, pltpu.roll(re, NF, 1)).astype(BF16)
            spec_ref[t, 1] = jnp.where(lower, im, pltpu.roll(im, NF, 1)).astype(BF16)
        return carry

    lax.fori_loop(0, TILES // step, some_tiles, 0)


def form_spectra(mask_tiles, step=4):
    wave = wave_table()
    return pl.pallas_call(
        functools.partial(spectra_kernel, step),
        in_specs=[HBM] * 3,
        out_specs=VMEM,
        out_shape=jax.ShapeDtypeStruct((TILES, 2, NF, 2 * NF), BF16),
        scratch_shapes=[
            pltpu.VMEM((TILES, P_SIZE, P_SIZE), BF16),
            pltpu.VMEM((P_SIZE, 2 * NF), BF16),
            pltpu.VMEM((2 * NF, P_SIZE), BF16),
            pltpu.SemaphoreType.DMA((TILES,)),
            pltpu.SemaphoreType.DMA((2,)),
        ],
        name="spectra",
        cost_estimate=pl.CostEstimate(flops=10**9, bytes_accessed=5 * 10**6, transcendentals=0),
    )(mask_tiles, as_bf16(wave.T), as_bf16(wave))


def image_kernel(
    first_ref, second_ref, first_div_ref, second_div_ref, label_ref, centre_ref, height_ref,
    spec_hbm, right_hbm, *rest
):
    pieces, (out_ref, held, spec_ref, left_ref, right_ref, pair_ref, sems, table_sems) = rest[:8], rest[8:]
    tables = [
        pltpu.make_async_copy(source, target, table_sems.at[at])
        for at, (source, target) in enumerate(
            ((right_hbm, right_ref), (spec_hbm, spec_ref))
        )
    ]
    for table in tables:
        table.start()

    def fetch(tile, carry):
        set_id = label_ref[tile] // NSUP
        first = (first_ref[0] - (set_id // first_div_ref[0])) & 3
        second = (second_ref[0] - (set_id // second_div_ref[0])) & 3
        which = second * 2 + first // 2
        for at, ref in enumerate(pieces):

            @pl.when(which == at)
            def _():
                pltpu.make_async_copy(ref.at[first & 1], held.at[tile], sems.at[tile]).start()

        return carry

    lax.fori_loop(0, TILES, fetch, 0)
    heights = jnp.sum(height_ref[...], axis=0)
    mean = jnp.sum(heights, keepdims=True) * (1.0 / (SC * SC))
    height_row = lax.broadcasted_iota(jnp.int32, heights.shape, 0)
    height_lane = lax.broadcasted_iota(jnp.int32, heights.shape, 1)

    for table in tables:
        table.wait()
    left_ref[...] = right_ref[...].T
    for at in range(4):
        rows = slice(at * NF, (at + 1) * NF)
        block = right_ref[(at // 2) * NF : (at // 2 + 1) * NF]
        pair_ref[rows, (at % 2) * 2 * Q : (at % 2 + 1) * 2 * Q] = block
        pair_ref[rows, (1 - at % 2) * 2 * Q : (2 - at % 2) * 2 * Q] = jnp.zeros_like(block)

    def some_tiles(trip, carry):
        batch = [trip * 4 + at for at in range(4)]
        for t in batch:
            pltpu.make_async_copy(pieces[0].at[0], held.at[t], sems.at[t]).wait()
        for t in batch:
            cell = label_ref[t] & (NSUP - 1)
            row = cell // SC
            here = (height_row == (row & 7)) & (height_lane == (row // 8) * SC + (cell & (SC - 1)))
            shift = jnp.sum(jnp.where(here, heights, 0.0), keepdims=True) - mean
            shift = GAIN_SCALE * shift - centre_ref[label_ref[t] // NSUP]
            re_part = spec_ref[t, 0].astype(F32)
            im_part = spec_ref[t, 1].astype(F32)
            re_part = jnp.concatenate([re_part, re_part], axis=1)
            im_part = jnp.concatenate([im_part, im_part], axis=1)
            filtered = []
            for g in range(GROUPS):
                kern_re = held[t, g, 0].astype(F32) + shift * held[t, g, 2].astype(F32)
                kern_im = held[t, g, 1].astype(F32) + shift * held[t, g, 3].astype(F32)
                prod_re = kern_re * re_part - kern_im * im_part
                prod_im = kern_re * im_part + kern_im * re_part
                filtered.append(jnp.concatenate([prod_re.astype(BF16), prod_im.astype(BF16)], axis=0))
            along = jnp.dot(
                left_ref[...], jnp.concatenate(filtered, axis=1), preferred_element_type=F32
            ).astype(BF16)
            for rows in range(0, Q, Q // 2):
                both = [
                    jnp.concatenate(
                        [along[rows + half : rows + half + Q // 2, at : at + 2 * NF] for half in (0, Q)],
                        axis=1,
                    )
                    for at in range(0, GROUPS * 4 * NF, 2 * NF)
                ]
                fields = jnp.dot(jnp.concatenate(both, axis=0), pair_ref[...], preferred_element_type=F32)
                total = jnp.zeros((Q // 2, Q), F32)
                for at in range(0, GROUPS * Q, Q // 2):
                    for part in range(4):
                        block = fields[at : at + Q // 2, part * Q : (part + 1) * Q]
                        total = total + block * block
                out_ref[t, rows : rows + Q // 2] = total.astype(out_ref.dtype)
        return carry

    lax.fori_loop(0, TILES // 4, some_tiles, 0)


def image(place, labels, centre, heights, spectra, pieces):
    return pl.pallas_call(
        image_kernel,
        in_specs=[SMEM] * 6 + [VMEM, ANY, HBM] + [ANY] * 8,
        out_specs=VMEM,
        out_shape=jax.ShapeDtypeStruct((TILES, Q, Q), BF16),
        scratch_shapes=[
            pltpu.VMEM((TILES, GROUPS, 4, NF, 4 * NF), BF16),
            pltpu.VMEM((TILES, 2, NF, 2 * NF), BF16),
            pltpu.VMEM((2 * Q, 2 * NF), BF16),
            pltpu.VMEM((2 * NF, 2 * Q), BF16),
            pltpu.VMEM((4 * NF, 4 * Q), BF16),
            pltpu.SemaphoreType.DMA((TILES,)),
            pltpu.SemaphoreType.DMA((2,)),
        ],
        name="image",
        compiler_params=pltpu.CompilerParams(vmem_limit_bytes=16 << 20),
        cost_estimate=pl.CostEstimate(flops=3 * 10**9, bytes_accessed=4 * 10**6, transcendentals=0),
    )(*place, labels, centre, heights, spectra, as_bf16(image_table()), *pieces)


def resist_kernel(
    own_hbm, other_hbm, resist_hbm, resist_t_hbm, out_hbm,
    own_ref, other_ref, resist_ref, resist_t_ref, image_ref, sems, out_sems,
):
    copies = [
        pltpu.make_async_copy(source, target, sems.at[at])
        for at, (source, target) in enumerate(
            (
                (own_hbm, own_ref),
                (other_hbm, other_ref),
                (resist_t_hbm, resist_t_ref),
                (resist_hbm, resist_ref),
            )
        )
    ]
    for copy in copies:
        copy.start()
    for copy in copies:
        copy.wait()

    def some_tiles(trip, carry):
        at = pl.ds(trip * 2, 2)
        intensity = (own_ref[at].astype(F32) + other_ref[at].astype(F32)) * (1.0 / KER)
        intensity = intensity.astype(BF16).reshape(2 * Q, Q)
        half_way = jnp.dot(intensity, resist_t_ref[...], preferred_element_type=F32).astype(BF16)
        for t in range(2):
            image_ref[trip * 2 + t] = jnp.dot(
                resist_ref[...], half_way[t * Q : (t + 1) * Q], preferred_element_type=F32
            ).astype(BF16)
            out_copy(trip * 2 + t).start()
        return carry

    def out_copy(t):
        return pltpu.make_async_copy(image_ref.at[t], out_hbm.at[t], out_sems.at[t])

    lax.fori_loop(0, TILES // 2, some_tiles, 0)
    for t in range(TILES):
        out_copy(t).wait()


def resist(own, other):
    table = resist_table(P_SIZE, Q)
    return pl.pallas_call(
        resist_kernel,
        in_specs=[ANY, ANY, HBM, HBM],
        out_specs=ANY,
        out_shape=jax.ShapeDtypeStruct((TILES, P_SIZE, P_SIZE), BF16),
        scratch_shapes=[
            pltpu.VMEM((TILES, Q, Q), BF16),
            pltpu.VMEM((TILES, Q, Q), BF16),
            pltpu.VMEM((P_SIZE, Q), BF16),
            pltpu.VMEM((Q, P_SIZE), BF16),
            pltpu.VMEM((TILES, P_SIZE, P_SIZE), BF16),
            pltpu.SemaphoreType.DMA((4,)),
            pltpu.SemaphoreType.DMA((TILES,)),
        ],
        name="resist",
        compiler_params=pltpu.CompilerParams(vmem_limit_bytes=12 << 20),
        cost_estimate=pl.CostEstimate(flops=10**9, bytes_accessed=5 * 10**6, transcendentals=0),
    )(own, other, as_bf16(table), as_bf16(table.T))


PLACES = [(z, core, x, y) for z in range(4) for core in range(2) for x in range(4) for y in range(4)]


def place_of(z, core, x, y):
    return ((z * 2 + core) * 4 + x % 4) * 4 + y % 4


def ring(phase, step):
    pairs = []
    for z, core, x, y in PLACES:
        along_y = (core + phase) % 2 == 0
        to = (z, core, x, y + step) if along_y else (z, core, x + step, y)
        pairs.append((place_of(z, core, x, y), place_of(*to)))
    return pairs


def send(value, phase, step):
    return lax.ppermute(value, ALL, ring(phase, step))


def after_all(value, *others):
    return lax.optimization_barrier((value, *others))[0]


def partner(x):
    return lax.ppermute(x, "tile", [(t, t ^ 1) for t in range(8)])


def exchange(copies, axis):
    return lax.all_to_all(copies, axis, 0, 0, tiled=True)


def device_steps(mask_tiles, class_of_tile, cell_of_tile, kernels, class_center):
    core = lax.axis_index("tile") % 2
    focus = lax.axis_index("focus")
    x, y = focus // 4, focus % 4
    place = [
        jnp.reshape(value.astype(jnp.int32), (1,))
        for value in (
            jnp.where(core == 0, y, x),
            jnp.where(core == 0, x, y),
            jnp.where(core == 0, 1, 4),
            jnp.where(core == 0, 4, 1),
        )
    ]
    labels = class_of_tile[:, 0] * NSUP + cell_of_tile
    other_labels = partner(labels)

    mine = lax.dynamic_slice_in_dim(kernels[0], core * HALF, HALF, 0)
    mine = mine.reshape(GROUPS, 4, 4, NF, NF).transpose(0, 2, 3, 1, 4).reshape(GROUPS, 4, NF, 4 * NF)
    before = send(mine, 0, 1)
    after = send(mine, 0, -1)
    far = send(mine, 0, 2)
    heights = density_heights(mask_tiles, cell_of_tile, lax.axis_size("tile"))
    low = jnp.stack([mine, after_all(before, heights)])
    high = jnp.stack([after_all(far, heights), after])
    low_before = send(low, 1, 1)
    high_after = send(high, 1, -1)
    high_before = send(high, 1, 1)
    low_after = send(low, 1, -1)
    low_far = send(low_before, 1, 1)
    high_far = send(high_after, 1, -1)
    heights = jnp.sum(exchange(heights, "tile"), axis=0)
    heights = jnp.broadcast_to(heights[None], (lax.axis_size("focus"), *heights.shape))
    heights = exchange(heights, "focus")
    spectra = form_spectra(mask_tiles)
    other_spectra = partner(spectra)
    pieces = (low, high, low_before, high_before, low_far, high_far, low_after, high_after)
    other = image(place, other_labels, class_center, heights, other_spectra, pieces)
    other = partner(other)
    own = image(place, labels, class_center, heights, spectra, pieces)
    return resist(own, other)


def solution(mesh):
    placed = (
        P(("tile", "focus"), None, None),
        P(("tile", "focus"), None),
        P(("tile", "focus")),
        P("focus", None, None, None),
        P(),
    )
    return jax.shard_map(
        device_steps,
        mesh=mesh,
        in_specs=placed,
        out_specs=P(("tile", "focus"), None, None),
        check_vma=False,
    )
```
